768 devices in a mesh: region: 24 (over z, core), aux: 32 (over x, y).
Axes of the slice: x: 4, y: 8, z: 12, core: 2. Of those that a mesh axis runs over, the one named last changes fastest.
Arguments:
- occ_tiles: bfloat16 [384, 128, 128], P('region'), may hold values from -0.5 to 0.5
- vir_tiles: bfloat16 [384, 128, 128], P('region'), may hold values from -0.5 to 0.5
- three_index: bfloat16 [48, 64, 128, 128], P('region', 'aux'), may hold values from -6 to 6
- send_lists: int32 [24, 2, 48], P('region'), may hold values from 0 to 15
- term_pairs: int32 [24, 128, 2], P('region'), may hold values from 0 to 1
- term_tiles: int32 [24, 128, 2], P('region'), may hold values from 0 to 47
- term_count: int32 [24], P('region'), may hold values from 1 to 128, 1536 in all
- z_pattern: int32 [32, 32], P('aux'), may hold values 0 or 1
- laplace_point: int32 [1], replicated, may hold values from 0 to 7
Outputs:
- z_block: float32 [64, 64], P('aux')
The draws below stay inside these ranges and needn't reach their ends.
Inputs may be any that keep to these rules, and one draw needn't show every extreme that they name: `term_count`: the largest count is exactly 128; the counts sum to 1536.
All inputs are finite; a program needn't handle non-finite values. No bound on the sum of `term_count` or of `z_pattern` on one device may be relied on, other than what follows from the above.
Results may differ from the reference program's by a relative error of at most 0.0041.
Values may be sent and summed in bfloat16 or wider, within the bound.
No kernel may reach another device: no remote copies, remote signals or barrier semaphores. Data moves between devices by JAX's collectives and lax.ppermute only.
A program may use at most 32 MiB of HBM per device.

```python
import math
import jax
import jax.numpy as jnp
import numpy as np
from jax import lax

BS = 128
NTILE = 16
SLOT = 2
NPAIR = 2
PB = 2
NTERM = 128
REGIONS = 24
NAUXB = 64
PAIRS = 48
TILES = 384
RECV = 48
N_REGION = 24
N_AUX = 32


def plant(result, stream_key, smallest, largest):
    longest = result.shape.index(max(result.shape))
    spots = []
    for shift in (0, 1):
        where = [jax.random.randint(jax.random.fold_in(stream_key, axis), (), 0, length) for axis, length in enumerate(result.shape)]
        where[longest] = (where[longest] + shift) % result.shape[longest]
        spots.append(tuple(where))
    return result.at[spots[0]].set(smallest).at[spots[1]].set(largest)


def block_levels(rng, dims, cuts, smallest, high):
    level, own = 1.0, jax.random.fold_in(rng, 6)
    for dim, shards_of in cuts:
        heights = jnp.exp(jax.random.uniform(jax.random.fold_in(own, dim), (shards_of,), jnp.float32, smallest / len(cuts), high / len(cuts)))
        level = level * jnp.repeat(heights, dims[dim] // shards_of).reshape([-1 if axis == dim else 1 for axis in range(len(dims))])
    return level


def split_up(amount, total, reach, lean):
    weights = [(1 << 20) // math.isqrt(rank ** lean) + 1 for rank in range(2, amount + 1)]
    surplus, counts = total - reach - (amount - 1), [1] * (amount - 1)
    while surplus > 0:
        candidates = [i for i in range(amount - 1) if counts[i] < reach]
        whole, remaining = sum([weights[i] for i in candidates]), surplus
        for i in candidates:
            extra = min(reach - counts[i], max(1, remaining * weights[i] // whole), surplus)
            counts[i] = counts[i] + extra
            surplus = surplus - extra
    return np.array([reach] + counts)


def uneven(stream_key, count, total, limit, slope):
    if count == 2:
        one = jax.random.randint(stream_key, (), max(1, total - limit), min(limit, total - 1) + 1)
        return jnp.stack([one, total - one])
    lengths = jnp.asarray(split_up(count, total, limit, slope), jnp.int32)
    couples = (count - 1) // 2
    giver, sink = lengths[1:1 + 2 * couples:2], lengths[2:2 + 2 * couples:2]
    room = jnp.minimum(giver - 1, limit - sink)
    moved = jax.random.randint(jax.random.fold_in(stream_key, 1), (couples,), 0, 1 << 20) % (room + 1)
    lengths = lengths.at[1:1 + 2 * couples:2].set(giver - moved).at[2:2 + 2 * couples:2].set(sink + moved)
    return lengths[jax.random.permutation(jax.random.fold_in(stream_key, 2), count)]


def bell_draw(key, dims, spread, reach, pieces=(), kind=jnp.bfloat16):
    result = jax.random.normal(key, dims, jnp.float32) * spread
    if len(pieces) > 0:
        result = block_levels(key, dims, pieces, -0.22, 0.18) * result
    return jnp.clip(result, min=-reach, max=reach).astype(kind)


def setup_inputs(seed: int = 0) -> dict:
    streams_of = jax.random.split(jax.random.key(seed), 10)
    occ_tiles = bell_draw(streams_of[0], (TILES, BS, BS), BS ** -0.5, 0.5, ((0, 24),))
    vir_tiles = bell_draw(streams_of[1], (TILES, BS, BS), BS ** -0.5, 0.5, ((0, 24),))
    three_index = bell_draw(streams_of[2], (PAIRS, NAUXB, BS, BS), 1.0, 6.0, ((0, 24), (1, 32)))
    send_lists = plant(jax.random.randint(streams_of[3], (REGIONS, 2, RECV), 0, NTILE), jax.random.fold_in(streams_of[3], 1), 0, NTILE - 1).astype(jnp.int32)
    term_pairs = plant(jax.random.randint(streams_of[4], (REGIONS, NTERM, 2), 0, NPAIR), jax.random.fold_in(streams_of[4], 1), 0, NPAIR - 1).astype(jnp.int32)
    term_tiles = plant(jax.random.randint(streams_of[5], (REGIONS, NTERM, 2), 0, RECV), jax.random.fold_in(streams_of[5], 1), 0, RECV - 1).astype(jnp.int32)
    term_count = uneven(streams_of[6], REGIONS, NTERM * N_REGION // 2, NTERM, 2).astype(jnp.int32)
    z_pattern = plant((jax.random.randint(streams_of[7], (N_AUX, N_AUX), 0, 4) < 3).astype(jnp.int32), jax.random.fold_in(streams_of[7], 1), 0, 1)
    laplace_point = jax.random.randint(streams_of[8], (1,), 0, 8).astype(jnp.int32)
    return dict(occ_tiles=occ_tiles, vir_tiles=vir_tiles, three_index=three_index, send_lists=send_lists, term_pairs=term_pairs, term_tiles=term_tiles, term_count=term_count, z_pattern=z_pattern, laplace_point=laplace_point)


def fetch(store, send_lists, which):
    regions = N_REGION
    local = send_lists[:, which, :].reshape(regions, regions, SLOT)
    offset = (jnp.arange(regions, dtype=jnp.int32) * NTILE).astype(jnp.int32)
    glob = (local + offset[:, None, None]).astype(jnp.int32)
    glob = jnp.transpose(glob, (1, 0, 2)).reshape(regions, regions * SLOT)
    return store[glob]

def region_wide(occ_recv, vir_recv, blocks, pairs, tiles, count):
    hi = lax.Precision.HIGHEST
    block_len = 8
    target = jnp.arange(NPAIR, dtype=jnp.int32)

    def step(acc, index):
        start = (index * block_len).astype(jnp.int32)
        pair_blk = lax.dynamic_slice_in_dim(pairs, start, block_len, 0)
        tile_blk = lax.dynamic_slice_in_dim(tiles, start, block_len, 0)
        live = start + jnp.arange(block_len, dtype=jnp.int32) < count
        occ = occ_recv[tile_blk[:, 0]].astype(jnp.float32)
        vir = vir_recv[tile_blk[:, 1]].astype(jnp.float32)
        source = blocks[pair_blk[:, 1]].astype(jnp.float32)
        half = jnp.einsum('tij,tpjk->tpik', occ, source, precision=hi).astype(jnp.bfloat16)
        second = jnp.einsum('tpik,tkl->tpil', half.astype(jnp.float32), vir, precision=hi)
        onehot = ((pair_blk[:, 0][None, :] == target[:, None]) & live[None, :]).astype(jnp.float32)
        return (acc + jnp.einsum('nt,tpil->npil', onehot, second, precision=hi), None)
    init = jnp.zeros((NPAIR, NAUXB, BS, BS), jnp.float32)
    acc, unused = lax.scan(step, init, jnp.arange(NTERM // 8, dtype=jnp.int32))
    return acc.astype(jnp.bfloat16)

def reference(occ_tiles, vir_tiles, three_index, send_lists, term_pairs, term_tiles, term_count, z_pattern, laplace_point):
    occ_recv = fetch(occ_tiles, send_lists, 0)
    vir_recv = fetch(vir_tiles, send_lists, 1)
    blocks = three_index.reshape(N_REGION, NPAIR, NAUXB, BS, BS)

    def one_region(items):
        occ, vir, blk, pairs, tiles, count = items
        wide = region_wide(occ, vir, blk, pairs, tiles, count)
        return jnp.einsum('npij,nqij->pq', blk.astype(jnp.float32), wide.astype(jnp.float32), precision=lax.Precision.HIGHEST)
    parts = lax.map(one_region, (occ_recv, vir_recv, blocks, term_pairs, term_tiles, term_count))
    raw = lax.optimization_barrier(jnp.sum(parts, axis=0))
    mask = jnp.repeat(jnp.repeat(z_pattern, PB, axis=0), PB, axis=1).astype(jnp.float32)
    weight = 0.5 + 0.125 * laplace_point[0].astype(jnp.float32)
    scale = weight / (BS * jnp.sqrt(jnp.float32(REGIONS * NTERM)))
    return raw * mask * scale
```

```python
import jax
import jax.numpy as jnp
from jax import lax
from jax.experimental import pallas as pl
from jax.experimental.pallas import tpu as pltpu
from jax.sharding import PartitionSpec as P

NX = 4
NY = 8
NI = 4
NL = 2
WIDTH = 128
IB = WIDTH // NI
LB = WIDTH // NL
Y_GROUPS = [[x * NY + y for y in range(NY)] for x in range(NX)]
X_GROUPS = [[x * NY + y for x in range(NX)] for y in range(NY)]


def pick_kernel(spots, lists, occ, vir, out):
    row = spots[0] * IB
    col = spots[1] * LB
    r = lax.broadcasted_iota(jnp.int32, (2 * WIDTH, WIDTH), 0)
    c = lax.broadcasted_iota(jnp.int32, (2 * WIDTH, WIDTH), 1)
    wanted = jnp.where(c < LB, c + col, c - LB + WIDTH + col)
    select = jnp.where(r == wanted, 1.0, 0.0).astype(jnp.bfloat16)
    for d in range(out.shape[0]):
        for j in range(2):
            out[d, j * IB : (j + 1) * IB, :] = occ[lists[0, 2 * d + j], pl.ds(pl.multiple_of(row, IB), IB), :]
        pair = jnp.concatenate([vir[lists[1, 2 * d]], vir[lists[1, 2 * d + 1]]], axis=1)
        out[d, 2 * IB :, :] = jnp.dot(pair, select, preferred_element_type=jnp.float32).astype(
            jnp.bfloat16
        )


def pick(spots, lists, occ, vir, regions):
    smem = pl.BlockSpec(memory_space=pltpu.SMEM)
    vmem = pl.BlockSpec(memory_space=pltpu.VMEM)
    return pl.pallas_call(
        pick_kernel,
        out_shape=jax.ShapeDtypeStruct((regions, 2 * IB + WIDTH, WIDTH), jnp.bfloat16),
        in_specs=[smem, smem, vmem, vmem],
        out_specs=vmem,
        compiler_params=pltpu.CompilerParams(vmem_limit_bytes=16 << 20),
        cost_estimate=pl.CostEstimate(flops=2 * 24 * 128 * 256 * 128, bytes_accessed=3 << 20, transcendentals=0),
    )(spots, lists, occ, vir)


CHUNK = 4


def transform_kernel(pairs, tiles, count, recv, bq, bp, out, half, acc, wide, order, number):
    regions = recv.shape[0]
    nq = bq.shape[0] * bq.shape[2]
    rows = nq * IB
    number[0] = 0
    number[1] = 0

    def place(t, carry):
        p = pairs[t, 0]
        n = number[p]
        order[p, 0, n] = pairs[t, 1] * (2 * regions) + tiles[t, 0]
        order[p, 1, n] = tiles[t, 1]
        number[p] = n + 1
        return carry

    lax.fori_loop(0, count[0], place, 0)

    group = 4

    def first(step, carry):
        q = step // bq.shape[0]
        y = step % bq.shape[0]
        source = jnp.concatenate([bq[y, q, 0], bq[y, q, 1]], axis=1)
        for s in range(0, regions, group):
            occ = recv[s : s + group, 0 : 2 * IB, :].reshape(group * 2 * IB, WIDTH)
            res = jnp.dot(occ, source, preferred_element_type=jnp.float32).astype(jnp.bfloat16)
            for u in range(2 * group):
                for f in range(2):
                    start = pl.multiple_of((y * 2 + f) * IB, IB)
                    half[q * (2 * regions) + 2 * s + u, pl.ds(start, IB), :] = res[
                        u * IB : (u + 1) * IB, f * WIDTH : (f + 1) * WIDTH
                    ]
        return carry

    lax.fori_loop(0, 2 * bq.shape[0], first, 0)

    lane = lax.broadcasted_iota(jnp.int32, (WIDTH, WIDTH), 1)
    for p in range(2):
        acc[p] = jnp.zeros((rows, WIDTH), jnp.float32)
        live = number[p]

        def second(step, carry, p=p, live=live):
            lhs = []
            rhs = []
            for u in range(CHUNK):
                t = step * CHUNK + u
                at = jnp.minimum(t, live - 1)
                b = order[p, 1, at]
                side = jnp.where(t < live, b % 2, 2)
                lhs.append(half[order[p, 0, at]])
                tile = recv[b // 2, 2 * IB :, :]
                rhs.append(jnp.where(lane // LB == side, tile, jnp.zeros_like(tile)))
            acc[p] += jnp.dot(
                jnp.concatenate(lhs, axis=1),
                jnp.concatenate(rhs, axis=0),
                preferred_element_type=jnp.float32,
            )
            return carry

        lax.fori_loop(0, (live + CHUNK - 1) // CHUNK, second, 0)
    low = acc[0]
    high = acc[1]
    lanes = lax.broadcasted_iota(jnp.int32, (rows, WIDTH), 1)
    wide[...] = jnp.where(
        lanes < LB, low + pltpu.roll(low, LB, 1), high + pltpu.roll(high, LB, 1)
    )
    flat = jnp.concatenate(
        [wide[pl.ds(i, nq, stride=IB), :].astype(jnp.bfloat16) for i in range(IB)], axis=1
    )
    out[...] = lax.dot_general(
        bp[...], flat, (((1,), (1,)), ((), ())), preferred_element_type=jnp.float32
    )


def transform(pairs, tiles, count, recv, bq, bp):
    smem = pl.BlockSpec(memory_space=pltpu.SMEM)
    vmem = pl.BlockSpec(memory_space=pltpu.VMEM)
    regions = recv.shape[0]
    nterms = pairs.shape[0]
    nq = bq.shape[0] * bq.shape[2]
    return pl.pallas_call(
        transform_kernel,
        out_shape=jax.ShapeDtypeStruct((bp.shape[0], nq), jnp.float32),
        in_specs=[smem, smem, smem, vmem, vmem, vmem],
        out_specs=vmem,
        scratch_shapes=[
            pltpu.VMEM((4 * regions, nq * IB, WIDTH), jnp.bfloat16),
            pltpu.VMEM((2, nq * IB, WIDTH), jnp.float32),
            pltpu.VMEM((nq * IB, WIDTH), jnp.float32),
            pltpu.SMEM((2, 2, nterms), jnp.int32),
            pltpu.SMEM((2,), jnp.int32),
        ],
        compiler_params=pltpu.CompilerParams(vmem_limit_bytes=40 << 20),
        cost_estimate=pl.CostEstimate(flops=4 << 30, bytes_accessed=4 << 20, transcendentals=0),
    )(pairs, tiles, count, recv, bq, bp)


def per_device(
    occ_tiles,
    vir_tiles,
    three_index,
    send_lists,
    term_pairs,
    term_tiles,
    term_count,
    z_pattern,
    laplace_point,
):
    regions = lax.axis_size("region")
    naux = lax.axis_size("aux")
    width = occ_tiles.shape[1]
    per_aux = three_index.shape[1]
    nterms = term_pairs.shape[1]
    nall = naux * per_aux
    aux = lax.axis_index("aux")
    x = aux // NY
    y = aux % NY
    spots = jnp.stack([y // NL, y % NL]).astype(jnp.int32)

    outgoing = pick(spots, send_lists[0], occ_tiles, vir_tiles, regions)
    recv = lax.all_to_all(outgoing, "region", 0, 0, tiled=True)

    bq = lax.all_gather(three_index, "aux", axis=0, tiled=False, axis_index_groups=Y_GROUPS)
    rows = lax.dynamic_slice_in_dim(bq, (y // NL) * IB, IB, 3)
    part = lax.dynamic_slice_in_dim(rows, (y % NL) * LB, LB, 4)
    part = jnp.concatenate([part[:, 0], part[:, 1]], axis=3)
    part = part.reshape(NY * per_aux, IB * WIDTH)
    bp = lax.all_gather(part, "aux", axis=0, tiled=True, axis_index_groups=X_GROUPS)

    partial = transform(term_pairs[0], term_tiles[0], term_count, recv, bq, bp)

    outs = partial.reshape(naux, per_aux, -1)
    spread = lax.all_to_all(outs, "aux", 0, 0, tiled=True)
    mine = jnp.sum(spread.reshape(NX, NY, per_aux, -1), axis=1)
    mine = jnp.transpose(mine, (1, 0, 2)).reshape(per_aux, nall)
    every = lax.all_to_all(
        jnp.broadcast_to(mine[None], (regions, per_aux, nall)), "region", 0, 0, tiled=True
    )
    summed = jnp.sum(every, axis=0)
    mask_row = jnp.repeat(z_pattern[0], per_aux).astype(jnp.float32)
    weight = 0.5 + 0.125 * laplace_point[0].astype(jnp.float32)
    scale = weight / (width * jnp.sqrt(jnp.float32(regions * nterms)))
    return summed * mask_row[None, :] * scale


def solution(mesh):
    in_specs = (
        P("region", None, None),
        P("region", None, None),
        P("region", "aux", None, None),
        P("region", None, None),
        P("region", None, None),
        P("region", None, None),
        P("region"),
        P("aux", None),
        P(),
    )
    out_specs = P("aux", None)
    return jax.shard_map(
        per_device, mesh=mesh, in_specs=in_specs, out_specs=out_specs, check_vma=False
    )
```

```python
import jax
import jax.numpy as jnp
from jax import lax
from jax.experimental import pallas as pl
from jax.experimental.pallas import tpu as pltpu
from jax.sharding import PartitionSpec as P

NX = 4
NY = 8
NI = 4
NL = 2
NG = NY // NL
WIDTH = 128
IB = WIDTH // NI
LB = WIDTH // NL
X_GROUPS = [[x * NY + y for x in range(NX)] for y in range(NY)]
PAIR_GROUPS = [[x * NY + NL * g + h for g in range(NG)] for x in range(NX) for h in range(NL)]
OTHER = [(x * NY + y, x * NY + (y ^ 1)) for x in range(NX) for y in range(NY)]


def placed(body, ins, outs, space, **extra):
    return pl.pallas_call(
        body,
        out_shape=outs,
        in_specs=[pl.BlockSpec(memory_space=m) for m in ins],
        out_specs=pl.BlockSpec(memory_space=space),
        **extra,
    )


PARTS = 4


def pick_kernel(spots, lists, occ, vir, out, rows, tiles, staged, sems):
    row = pl.multiple_of(spots[0] * IB, IB)
    col = spots[1] * LB
    ntile = occ.shape[0]
    copies = [pltpu.make_async_copy(occ.at[:, pl.ds(row, IB), :], rows, sems.at[0])]
    step = ntile // PARTS
    for u in range(PARTS):
        at = pl.ds(u * step, step)
        copies.append(pltpu.make_async_copy(vir.at[at], tiles.at[at], sems.at[1 + u]))
    for c in copies:
        c.start()
    r = lax.broadcasted_iota(jnp.int32, (2 * WIDTH, WIDTH), 0)
    c = lax.broadcasted_iota(jnp.int32, (2 * WIDTH, WIDTH), 1)
    wanted = jnp.where(c < LB, c + col, c - LB + WIDTH + col)
    select = jnp.where(r == wanted, 1.0, 0.0).astype(jnp.bfloat16)
    for c in copies:
        c.wait()
    regions = staged.shape[0]
    step = regions // PARTS
    sent = []
    for u in range(PARTS):
        for d in range(u * step, (u + 1) * step):
            for j in range(2):
                staged[d, j * IB : (j + 1) * IB, :] = rows[lists[0, 2 * d + j]]
            pair = jnp.concatenate([tiles[lists[1, 2 * d]], tiles[lists[1, 2 * d + 1]]], axis=1)
            staged[d, 2 * IB :, :] = jnp.dot(
                pair, select, preferred_element_type=jnp.float32
            ).astype(jnp.bfloat16)
        at = pl.ds(u * step, step)
        sent.append(pltpu.make_async_copy(staged.at[at], out.at[at], sems.at[1 + PARTS + u]))
        sent[-1].start()
    for c in sent:
        c.wait()


def pick(spots, lists, occ, vir, regions):
    smem, hbm = pltpu.SMEM, pltpu.HBM
    shape = (regions, 2 * IB + WIDTH, WIDTH)
    return placed(
        pick_kernel,
        [smem, smem, hbm, hbm],
        jax.ShapeDtypeStruct(shape, jnp.bfloat16),
        hbm,
        scratch_shapes=[
            pltpu.VMEM((occ.shape[0], IB, WIDTH), jnp.bfloat16),
            pltpu.VMEM(vir.shape, jnp.bfloat16),
            pltpu.VMEM(shape, jnp.bfloat16),
            pltpu.SemaphoreType.DMA((1 + 2 * PARTS,)),
        ],
        compiler_params=pltpu.CompilerParams(vmem_limit_bytes=60 << 20),
        cost_estimate=pl.CostEstimate(flops=40 << 20, bytes_accessed=2 << 20, transcendentals=0),
    )(spots, lists, occ, vir)


CHUNK = 4


def transform_kernel(
    spots, pairs, tiles, count, recv, own, other, bp, out, half, acc, wide, order, number
):
    regions = recv.shape[0]
    nq = 2 * own.shape[0] * own.shape[2]
    rows = nq * IB
    parity = spots[1]
    group_at = spots[2]
    number[0] = 0
    number[1] = 0

    def place(t, carry):
        p = pairs[t, 0]
        n = number[p]
        order[p, 0, n] = pairs[t, 1] * (2 * regions) + tiles[t, 0]
        order[p, 1, n] = tiles[t, 1]
        number[p] = n + 1
        return carry

    lax.fori_loop(0, count[0], place, 0)

    group = 4
    for o, bq in enumerate((own, other)):

        def first(step, carry, o=o, bq=bq):
            q = step // NX
            x = step % NX
            source = jnp.concatenate([bq[x, q, 0], bq[x, q, 1]], axis=1)
            spot = ((parity ^ o) * NX + x) * 2
            for s in range(0, regions, group):
                occ = recv[s : s + group, 0 : 2 * IB, :].reshape(group * 2 * IB, WIDTH)
                res = jnp.dot(occ, source, preferred_element_type=jnp.float32).astype(jnp.bfloat16)
                for u in range(2 * group):
                    for f in range(2):
                        start = pl.multiple_of((spot + f) * IB, IB)
                        half[q * (2 * regions) + 2 * s + u, pl.ds(start, IB), :] = res[
                            u * IB : (u + 1) * IB, f * WIDTH : (f + 1) * WIDTH
                        ]
            return carry

        lax.fori_loop(0, 2 * NX, first, 0)

    lane = lax.broadcasted_iota(jnp.int32, (WIDTH, WIDTH), 1)
    for p in range(2):
        acc[p] = jnp.zeros((rows, WIDTH), jnp.float32)
        live = number[p]

        def second(step, carry, p=p, live=live):
            lhs = []
            rhs = []
            for u in range(CHUNK):
                t = step * CHUNK + u
                at = jnp.minimum(t, live - 1)
                b = order[p, 1, at]
                side = jnp.where(t < live, b % 2, 2)
                lhs.append(half[order[p, 0, at]])
                tile = recv[b // 2, 2 * IB :, :]
                rhs.append(jnp.where(lane // LB == side, tile, jnp.zeros_like(tile)))
            acc[p] += jnp.dot(
                jnp.concatenate(lhs, axis=1),
                jnp.concatenate(rhs, axis=0),
                preferred_element_type=jnp.float32,
            )
            return carry

        lax.fori_loop(0, (live + CHUNK - 1) // CHUNK, second, 0)
    low = acc[0]
    high = acc[1]
    lanes = lax.broadcasted_iota(jnp.int32, (rows, WIDTH), 1)
    wide[...] = jnp.where(
        lanes < LB, low + pltpu.roll(low, LB, 1), high + pltpu.roll(high, LB, 1)
    )
    flat = jnp.concatenate(
        [wide[pl.ds(i, nq, stride=IB), :].astype(jnp.bfloat16) for i in range(IB)], axis=1
    )
    partial = lax.dot_general(
        bp[...], flat, (((1,), (1,)), ((), ())), preferred_element_type=jnp.float32
    )
    n = lax.broadcasted_iota(jnp.int32, (nq, WIDTH), 0)
    c = lax.broadcasted_iota(jnp.int32, (nq, WIDTH), 1)
    at = ((n // 2) % NX) * nq + group_at * (nq // NX) + (n // (2 * NX)) * 2 + n % 2
    line = jnp.zeros((bp.shape[0] // 2, WIDTH), jnp.float32)
    split = partial.reshape(NG, 2, 2 * NX, nq)
    for f in range(2):
        spread = jnp.where(c == at + f * bp.shape[0], 1.0, 0.0)
        line += jnp.dot(
            split[:, f].reshape(NG * 2 * NX, nq),
            spread,
            preferred_element_type=jnp.float32,
            precision=lax.Precision.HIGHEST,
        )
    for g in range(NG):
        for h in range(NL):
            for x in range(NX):
                row = (g * NL + h) * NX + x
                out[x * NY + g * NL + h] = line[row : row + 1, :]


def transform(spots, pairs, tiles, count, recv, own, other, bp):
    smem, vmem = pltpu.SMEM, pltpu.VMEM
    regions = recv.shape[0]
    nterms = pairs.shape[0]
    nq = 2 * own.shape[0] * own.shape[2]
    return placed(
        transform_kernel,
        [smem] * 4 + [vmem] * 4,
        jax.ShapeDtypeStruct((bp.shape[0] // 2, 1, 2 * bp.shape[0]), jnp.float32),
        vmem,
        scratch_shapes=[
            pltpu.VMEM((4 * regions, nq * IB, WIDTH), jnp.bfloat16),
            pltpu.VMEM((2, nq * IB, WIDTH), jnp.float32),
            pltpu.VMEM((nq * IB, WIDTH), jnp.float32),
            pltpu.SMEM((2, 2, nterms), jnp.int32),
            pltpu.SMEM((2,), jnp.int32),
        ],
        compiler_params=pltpu.CompilerParams(vmem_limit_bytes=40 << 20),
        cost_estimate=pl.CostEstimate(flops=4 << 30, bytes_accessed=4 << 20, transcendentals=0),
    )(spots, pairs, tiles, count, recv, own, other, bp)


def total_kernel(parts, out):
    out[...] = jnp.broadcast_to(jnp.sum(parts[...], axis=0, keepdims=True), out.shape)


def total(parts, copies):
    return placed(
        total_kernel,
        [pltpu.VMEM],
        jax.ShapeDtypeStruct((copies,) + parts.shape[1:], parts.dtype),
        pltpu.VMEM,
        compiler_params=pltpu.CompilerParams(vmem_limit_bytes=1 << 20),
    )(parts)


def finish_kernel(parts, factor, out):
    line = jnp.sum(parts[...], axis=0) * factor[...]
    n = out.shape[1]
    out[0:1, :] = line[:, :n]
    out[1:2, :] = line[:, n:]


def finish(parts, factor):
    return placed(
        finish_kernel,
        [pltpu.VMEM, pltpu.VMEM],
        jax.ShapeDtypeStruct((2, parts.shape[2] // 2), parts.dtype),
        pltpu.VMEM,
        compiler_params=pltpu.CompilerParams(vmem_limit_bytes=1 << 20),
    )(parts, factor)


def per_device(
    occ_tiles,
    vir_tiles,
    three_index,
    send_lists,
    term_pairs,
    term_tiles,
    term_count,
    z_pattern,
    laplace_point,
):
    regions = lax.axis_size("region")
    width = occ_tiles.shape[1]
    per_aux = three_index.shape[1]
    nterms = term_pairs.shape[1]
    aux = lax.axis_index("aux").astype(jnp.int32)
    x = aux // NY
    y = aux % NY
    parity = y % NL
    spots = jnp.stack([x, parity, y // NL])

    outgoing = pick(spots, send_lists[0], occ_tiles, vir_tiles, regions)
    recv = lax.all_to_all(outgoing, "region", 0, 0, tiled=True)

    own = lax.all_gather(three_index, "aux", axis=0, tiled=False, axis_index_groups=X_GROUPS)
    other = lax.ppermute(own, "aux", OTHER)

    def sliced(b):
        b = lax.dynamic_slice_in_dim(b, x * IB, IB, 3)
        b = lax.dynamic_slice_in_dim(b, parity * LB, LB, 4)
        return jnp.concatenate([b[:, 0], b[:, 1]], axis=3)

    mine, theirs = sliced(own), sliced(other)
    even = parity == 0
    both = jnp.stack([jnp.where(even, mine, theirs), jnp.where(even, theirs, mine)])
    part = jnp.transpose(both, (2, 0, 1, 3, 4)).reshape(per_aux * NL * NX, IB * WIDTH)
    bp = lax.all_gather(part, "aux", axis=0, tiled=True, axis_index_groups=PAIR_GROUPS)

    partial = transform(
        spots, term_pairs[0], term_tiles[0], term_count, recv, own, other, bp
    )

    mask_row = jnp.repeat(z_pattern[0], per_aux).astype(jnp.float32)
    weight = 0.5 + 0.125 * laplace_point[0].astype(jnp.float32)
    scale = weight / (width * jnp.sqrt(jnp.float32(regions * nterms)))
    factor = jnp.concatenate([mask_row, mask_row])[None] * scale

    spread = lax.all_to_all(partial, "aux", 0, 0, tiled=True)
    every = lax.all_to_all(total(spread, regions), "region", 0, 0, tiled=True)
    return finish(every, factor)


def solution(mesh):
    in_specs = (
        P("region", None, None),
        P("region", None, None),
        P("region", "aux", None, None),
        P("region", None, None),
        P("region", None, None),
        P("region", None, None),
        P("region"),
        P("aux", None),
        P(),
    )
    out_specs = P("aux", None)
    return jax.shard_map(
        per_device, mesh=mesh, in_specs=in_specs, out_specs=out_specs, check_vma=False
    )
```

```python
import jax
import jax.numpy as jnp
from jax import lax
from jax.experimental import pallas as pl
from jax.experimental.pallas import tpu as pltpu
from jax.sharding import PartitionSpec as P

NX = 4
NY = 8
NI = 4
NL = 2
NG = NY // NL
WIDTH = 128
IB = WIDTH // NI
LB = WIDTH // NL
X_GROUPS = [[x * NY + y for x in range(NX)] for y in range(NY)]
PAIR_GROUPS = [[x * NY + NL * g + h for g in range(NG)] for x in range(NX) for h in range(NL)]
OTHER = [(x * NY + y, x * NY + (y ^ 1)) for x in range(NX) for y in range(NY)]


def placed(body, ins, outs, space, **extra):
    return pl.pallas_call(
        body,
        out_shape=outs,
        in_specs=[pl.BlockSpec(memory_space=m) for m in ins],
        out_specs=pl.BlockSpec(memory_space=space),
        **extra,
    )


def member():
    aux = lax.axis_index("aux")
    return aux // NY, aux % NY


PARTS = 4


def pick_kernel(lists, occ, vir, out, rows, tiles, staged, sems):
    x, y = member()
    row = pl.multiple_of(x * IB, IB)
    col = (y % NL) * LB
    ntile = occ.shape[0]
    copies = [pltpu.make_async_copy(occ.at[:, pl.ds(row, IB), :], rows, sems.at[0])]
    step = ntile // PARTS
    for u in range(PARTS):
        at = pl.ds(u * step, step)
        copies.append(pltpu.make_async_copy(vir.at[at], tiles.at[at], sems.at[1 + u]))
    for c in copies:
        c.start()
    r = lax.broadcasted_iota(jnp.int32, (2 * WIDTH, WIDTH), 0)
    c = lax.broadcasted_iota(jnp.int32, (2 * WIDTH, WIDTH), 1)
    wanted = jnp.where(c < LB, c + col, c - LB + WIDTH + col)
    select = jnp.where(r == wanted, 1.0, 0.0).astype(jnp.bfloat16)
    for c in copies:
        c.wait()
    regions = staged.shape[0]
    step = regions // PARTS
    sent = []
    for u in range(PARTS):
        for d in range(u * step, (u + 1) * step):
            for j in range(2):
                staged[d, j * IB : (j + 1) * IB, :] = rows[lists[0, 2 * d + j]]
            pair = jnp.concatenate([tiles[lists[1, 2 * d]], tiles[lists[1, 2 * d + 1]]], axis=1)
            staged[d, 2 * IB :, :] = jnp.dot(
                pair, select, preferred_element_type=jnp.float32
            ).astype(jnp.bfloat16)
        at = pl.ds(u * step, step)
        sent.append(pltpu.make_async_copy(staged.at[at], out.at[at], sems.at[1 + PARTS + u]))
        sent[-1].start()
    for c in sent:
        c.wait()


def pick(lists, occ, vir, regions):
    smem, hbm = pltpu.SMEM, pltpu.HBM
    shape = (regions, 2 * IB + WIDTH, WIDTH)
    return placed(
        pick_kernel,
        [smem, hbm, hbm],
        jax.ShapeDtypeStruct(shape, jnp.bfloat16),
        hbm,
        scratch_shapes=[
            pltpu.VMEM((occ.shape[0], IB, WIDTH), jnp.bfloat16),
            pltpu.VMEM(vir.shape, jnp.bfloat16),
            pltpu.VMEM(shape, jnp.bfloat16),
            pltpu.SemaphoreType.DMA((1 + 2 * PARTS,)),
        ],
        compiler_params=pltpu.CompilerParams(vmem_limit_bytes=60 << 20),
        cost_estimate=pl.CostEstimate(flops=40 << 20, bytes_accessed=2 << 20, transcendentals=0),
    )(lists, occ, vir)


GROUP = 2
WIDE = 2
CHUNK = 32


def transform_kernel(
    pairs, tiles, count, recv, own, other, same, rest, out, half, acc, wide
):
    regions = recv.shape[0]
    nq = 2 * own.shape[0] * own.shape[2]
    rows = nq * IB
    y = member()[1]
    parity = y % NL

    def first(n, carry):
        q = n // (NX // WIDE)
        at = (n % (NX // WIDE)) * WIDE
        source = jnp.concatenate(
            [bq[at + v, q, f] for v in range(WIDE) for bq in (own, other) for f in range(2)], axis=1
        )
        for s in range(0, regions, GROUP):
            occ = recv[s : s + GROUP, 0 : 2 * IB, :].reshape(GROUP * 2 * IB, WIDTH)
            res = jnp.dot(occ, source, preferred_element_type=jnp.float32).astype(jnp.bfloat16)
            for v in range(WIDE):
                for o in range(2):
                    for f in range(2):
                        spot = ((parity ^ o) * NX + at + v) * 2 + f
                        start = pl.multiple_of(spot * IB, IB)
                        left = (v * 4 + o * 2 + f) * WIDTH
                        for u in range(2 * GROUP):
                            half[q * (2 * regions) + 2 * s + u, pl.ds(start, IB), :] = res[
                                u * IB : (u + 1) * IB, left : left + WIDTH
                            ]
        return carry

    lax.fori_loop(0, 2 * NX // WIDE, first, 0)

    acc[...] = jnp.zeros_like(acc)
    live = count[0]
    lane = lax.broadcasted_iota(jnp.int32, (WIDTH, 2 * WIDTH), 1) // LB

    def second(n, carry):
        lhs = []
        rhs = []
        for u in range(CHUNK):
            t = n * CHUNK + u
            at = jnp.minimum(t, live - 1)
            b = tiles[at, 1]
            side = jnp.where(t < live, pairs[at, 0] * NL + b % 2, -1)
            lhs.append(half[pairs[at, 1] * (2 * regions) + tiles[at, 0]])
            tile = recv[b // 2, 2 * IB :, :]
            tile = jnp.concatenate([tile, tile], axis=1)
            rhs.append(jnp.where(lane == side, tile, jnp.zeros_like(tile)))
        acc[...] += jnp.dot(
            jnp.concatenate(lhs, axis=1),
            jnp.concatenate(rhs, axis=0),
            preferred_element_type=jnp.float32,
        )
        return carry

    lax.fori_loop(0, (live + CHUNK - 1) // CHUNK, second, 0)
    low = acc[:, :WIDTH]
    high = acc[:, WIDTH:]
    lanes = lax.broadcasted_iota(jnp.int32, (rows, WIDTH), 1)
    wide[...] = jnp.where(
        lanes < LB, low + pltpu.roll(low, LB, 1), high + pltpu.roll(high, LB, 1)
    )
    flat = jnp.concatenate(
        [wide[pl.ds(i, nq, stride=IB), :].astype(jnp.bfloat16) for i in range(IB)], axis=1
    )
    nall = 2 * same.shape[0]
    n = lax.broadcasted_iota(jnp.int32, (nq, WIDTH), 0)
    c = lax.broadcasted_iota(jnp.int32, (nq, WIDTH), 1)
    at = ((n // 2) % NX) * nq + (y // NL) * (nq // NX) + (n // (2 * NX)) * 2 + n % 2
    places = [jnp.where(c == at + f * nall, 1.0, 0.0) for f in range(2)]
    for o, bp in enumerate((same, rest)):
        partial = lax.dot_general(
            bp[...], flat, (((1,), (1,)), ((), ())), preferred_element_type=jnp.float32
        )
        lines = [
            jnp.dot(
                partial,
                place,
                preferred_element_type=jnp.float32,
                precision=lax.Precision.HIGHEST,
            )
            for place in places
        ]
        for g in range(NG):
            for v in range(NX):
                row = 2 * (g * NX + v)
                out[v * NY + NL * g + (parity ^ o)] = (
                    lines[0][row : row + 1, :] + lines[1][row + 1 : row + 2, :]
                )


def transform(pairs, tiles, count, recv, own, other, same, rest):
    smem, vmem = pltpu.SMEM, pltpu.VMEM
    regions = recv.shape[0]
    nq = 2 * own.shape[0] * own.shape[2]
    return placed(
        transform_kernel,
        [smem] * 3 + [vmem] * 5,
        jax.ShapeDtypeStruct((same.shape[0], 1, 4 * same.shape[0]), jnp.float32),
        vmem,
        scratch_shapes=[
            pltpu.VMEM((4 * regions, nq * IB, WIDTH), jnp.bfloat16),
            pltpu.VMEM((nq * IB, 2 * WIDTH), jnp.float32),
            pltpu.VMEM((nq * IB, WIDTH), jnp.float32),
        ],
        compiler_params=pltpu.CompilerParams(vmem_limit_bytes=40 << 20),
        cost_estimate=pl.CostEstimate(flops=4 << 30, bytes_accessed=4 << 20, transcendentals=0),
    )(pairs, tiles, count, recv, own, other, same, rest)


def total_kernel(parts, out):
    out[...] = jnp.broadcast_to(jnp.sum(parts[...], axis=0, keepdims=True), out.shape)


def total(parts, copies):
    return placed(
        total_kernel,
        [pltpu.VMEM],
        jax.ShapeDtypeStruct((copies,) + parts.shape[1:], parts.dtype),
        pltpu.VMEM,
        compiler_params=pltpu.CompilerParams(vmem_limit_bytes=1 << 20),
    )(parts)


def finish_kernel(parts, factor, out):
    line = jnp.sum(parts[...], axis=0) * factor[...]
    n = out.shape[1]
    out[0:1, :] = line[:, :n]
    out[1:2, :] = line[:, n:]


def finish(parts, factor):
    return placed(
        finish_kernel,
        [pltpu.VMEM, pltpu.VMEM],
        jax.ShapeDtypeStruct((2, parts.shape[2] // 2), parts.dtype),
        pltpu.VMEM,
        compiler_params=pltpu.CompilerParams(vmem_limit_bytes=1 << 20),
    )(parts, factor)


def per_device(
    occ_tiles,
    vir_tiles,
    three_index,
    send_lists,
    term_pairs,
    term_tiles,
    term_count,
    z_pattern,
    laplace_point,
):
    regions = lax.axis_size("region")
    width = occ_tiles.shape[1]
    per_aux = three_index.shape[1]
    nterms = term_pairs.shape[1]
    x, y = member()

    outgoing = pick(send_lists[0], occ_tiles, vir_tiles, regions)
    recv = lax.all_to_all(outgoing, "region", 0, 0, tiled=True)

    own = lax.all_gather(three_index, "aux", axis=0, tiled=False, axis_index_groups=X_GROUPS)
    other = lax.ppermute(own, "aux", OTHER)

    def sliced(b):
        b = lax.dynamic_slice_in_dim(b, x * IB, IB, 3)
        b = lax.dynamic_slice_in_dim(b, (y % NL) * LB, LB, 4)
        b = jnp.concatenate([b[:, 0], b[:, 1]], axis=3)
        return b.reshape(NX * per_aux, IB * WIDTH)

    def spread(b):
        return lax.all_gather(b, "aux", axis=0, tiled=True, axis_index_groups=PAIR_GROUPS)

    same = spread(sliced(own))
    theirs, same = lax.optimization_barrier((sliced(other), same))
    rest = spread(theirs)

    partial = transform(
        term_pairs[0], term_tiles[0], term_count, recv, own, other, same, rest
    )

    mask_row = jnp.repeat(z_pattern[0], per_aux).astype(jnp.float32)
    weight = 0.5 + 0.125 * laplace_point[0].astype(jnp.float32)
    scale = weight / (width * jnp.sqrt(jnp.float32(regions * nterms)))
    factor = jnp.concatenate([mask_row, mask_row])[None] * scale

    spread = lax.all_to_all(partial, "aux", 0, 0, tiled=True)
    every = lax.all_to_all(total(spread, regions), "region", 0, 0, tiled=True)
    return finish(every, factor)


def solution(mesh):
    in_specs = (
        P("region", None, None),
        P("region", None, None),
        P("region", "aux", None, None),
        P("region", None, None),
        P("region", None, None),
        P("region", None, None),
        P("region"),
        P("aux", None),
        P(),
    )
    out_specs = P("aux", None)
    return jax.shard_map(
        per_device, mesh=mesh, in_specs=in_specs, out_specs=out_specs, check_vma=False
    )
```

```python
import jax
import jax.numpy as jnp
from jax import lax
from jax.experimental import pallas as pl
from jax.experimental.pallas import tpu as pltpu
from jax.sharding import PartitionSpec as P

NX = 4
NY = 8
NI = 4
NL = 2
NG = NY // NL
WIDTH = 128
IB = WIDTH // NI
LB = WIDTH // NL
X_GROUPS = [[x * NY + y for x in range(NX)] for y in range(NY)]
OTHER = [(x * NY + y, x * NY + (y ^ 1)) for x in range(NX) for y in range(NY)]
HOPS = (2, 1, NG - 1)


def onward(hop):
    return [(x * NY + y, x * NY + (y + NL * hop) % NY) for x in range(NX) for y in range(NY)]


def placed(body, ins, outs, space, **extra):
    return pl.pallas_call(
        body,
        out_shape=outs,
        in_specs=[pl.BlockSpec(memory_space=m) for m in ins],
        out_specs=pl.BlockSpec(memory_space=space),
        **extra,
    )


def member():
    aux = lax.axis_index("aux")
    return aux // NY, aux % NY


PARTS = 4


def pick_kernel(lists, occ, vir, out, rows, tiles, staged, sems):
    x, y = member()
    row = pl.multiple_of(x * IB, IB)
    col = (y % NL) * LB
    ntile = occ.shape[0]
    copies = [pltpu.make_async_copy(occ.at[:, pl.ds(row, IB), :], rows, sems.at[0])]
    step = ntile // PARTS
    for u in range(PARTS):
        at = pl.ds(u * step, step)
        copies.append(pltpu.make_async_copy(vir.at[at], tiles.at[at], sems.at[1 + u]))
    for c in copies:
        c.start()
    r = lax.broadcasted_iota(jnp.int32, (2 * WIDTH, WIDTH), 0)
    c = lax.broadcasted_iota(jnp.int32, (2 * WIDTH, WIDTH), 1)
    wanted = jnp.where(c < LB, c + col, c - LB + WIDTH + col)
    select = jnp.where(r == wanted, 1.0, 0.0).astype(jnp.bfloat16)
    for c in copies:
        c.wait()
    regions = staged.shape[0]
    step = regions // PARTS
    sent = []
    for u in range(PARTS):
        for d in range(u * step, (u + 1) * step):
            for j in range(2):
                staged[d, j * IB : (j + 1) * IB, :] = rows[lists[0, 2 * d + j]]
            pair = jnp.concatenate([tiles[lists[1, 2 * d]], tiles[lists[1, 2 * d + 1]]], axis=1)
            staged[d, 2 * IB :, :] = jnp.dot(
                pair, select, preferred_element_type=jnp.float32
            ).astype(jnp.bfloat16)
        at = pl.ds(u * step, step)
        sent.append(pltpu.make_async_copy(staged.at[at], out.at[at], sems.at[1 + PARTS + u]))
        sent[-1].start()
    for c in sent:
        c.wait()


def pick(lists, occ, vir, regions):
    smem, hbm = pltpu.SMEM, pltpu.HBM
    shape = (regions, 2 * IB + WIDTH, WIDTH)
    return placed(
        pick_kernel,
        [smem, hbm, hbm],
        jax.ShapeDtypeStruct(shape, jnp.bfloat16),
        hbm,
        scratch_shapes=[
            pltpu.VMEM((occ.shape[0], IB, WIDTH), jnp.bfloat16),
            pltpu.VMEM(vir.shape, jnp.bfloat16),
            pltpu.VMEM(shape, jnp.bfloat16),
            pltpu.SemaphoreType.DMA((1 + 2 * PARTS,)),
        ],
        compiler_params=pltpu.CompilerParams(vmem_limit_bytes=60 << 20),
        cost_estimate=pl.CostEstimate(flops=40 << 20, bytes_accessed=2 << 20, transcendentals=0),
    )(lists, occ, vir)


GROUP = 2
WIDE = 2
CHUNK = 32


def transform_kernel(pairs, tiles, count, recv, own, other, out, half, acc, wide):
    regions = recv.shape[0]
    nq = 2 * own.shape[0] * own.shape[2]
    rows = nq * IB
    y = member()[1]
    parity = y % NL

    def first(n, carry):
        q = n // (NX // WIDE)
        at = (n % (NX // WIDE)) * WIDE
        source = jnp.concatenate(
            [bq[at + v, q, f] for v in range(WIDE) for bq in (own, other) for f in range(2)], axis=1
        )
        for s in range(0, regions, GROUP):
            occ = recv[s : s + GROUP, 0 : 2 * IB, :].reshape(GROUP * 2 * IB, WIDTH)
            res = jnp.dot(occ, source, preferred_element_type=jnp.float32).astype(jnp.bfloat16)
            for v in range(WIDE):
                for o in range(2):
                    for f in range(2):
                        spot = ((parity ^ o) * NX + at + v) * 2 + f
                        start = pl.multiple_of(spot * IB, IB)
                        left = (v * 4 + o * 2 + f) * WIDTH
                        for u in range(2 * GROUP):
                            half[q * (2 * regions) + 2 * s + u, pl.ds(start, IB), :] = res[
                                u * IB : (u + 1) * IB, left : left + WIDTH
                            ]
        return carry

    lax.fori_loop(0, 2 * NX // WIDE, first, 0)

    acc[...] = jnp.zeros_like(acc)
    live = count[0]
    lane = lax.broadcasted_iota(jnp.int32, (WIDTH, 2 * WIDTH), 1) // LB

    def second(n, carry):
        lhs = []
        rhs = []
        for u in range(CHUNK):
            t = n * CHUNK + u
            at = jnp.minimum(t, live - 1)
            b = tiles[at, 1]
            side = jnp.where(t < live, pairs[at, 0] * NL + b % 2, -1)
            lhs.append(half[pairs[at, 1] * (2 * regions) + tiles[at, 0]])
            tile = recv[b // 2, 2 * IB :, :]
            tile = jnp.concatenate([tile, tile], axis=1)
            rhs.append(jnp.where(lane == side, tile, jnp.zeros_like(tile)))
        acc[...] += jnp.dot(
            jnp.concatenate(lhs, axis=1),
            jnp.concatenate(rhs, axis=0),
            preferred_element_type=jnp.float32,
        )
        return carry

    lax.fori_loop(0, (live + CHUNK - 1) // CHUNK, second, 0)
    low = acc[:, :WIDTH]
    high = acc[:, WIDTH:]
    lanes = lax.broadcasted_iota(jnp.int32, (rows, WIDTH), 1)
    wide[...] = jnp.where(
        lanes < LB, low + pltpu.roll(low, LB, 1), high + pltpu.roll(high, LB, 1)
    )
    for i in range(IB):
        out[:, i * WIDTH : (i + 1) * WIDTH] = wide[pl.ds(i, nq, stride=IB), :].astype(jnp.bfloat16)


def transform(pairs, tiles, count, recv, own, other):
    smem, vmem = pltpu.SMEM, pltpu.VMEM
    regions = recv.shape[0]
    nq = 2 * own.shape[0] * own.shape[2]
    return placed(
        transform_kernel,
        [smem] * 3 + [vmem] * 3,
        jax.ShapeDtypeStruct((nq, IB * WIDTH), jnp.bfloat16),
        vmem,
        scratch_shapes=[
            pltpu.VMEM((4 * regions, nq * IB, WIDTH), jnp.bfloat16),
            pltpu.VMEM((nq * IB, 2 * WIDTH), jnp.float32),
            pltpu.VMEM((nq * IB, WIDTH), jnp.float32),
        ],
        compiler_params=pltpu.CompilerParams(vmem_limit_bytes=40 << 20),
        cost_estimate=pl.CostEstimate(flops=8 << 30, bytes_accessed=4 << 20, transcendentals=0),
    )(pairs, tiles, count, recv, own, other)


def contract_kernel(flat, *refs):
    parts, out = refs[:-1], refs[-1]
    y = member()[1]
    group = y // NL
    nq = flat.shape[0]
    nall = nq * NG
    partial = lax.dot_general(
        jnp.concatenate([p[...] for p in parts], axis=0),
        flat[...],
        (((1,), (1,)), ((), ())),
        preferred_element_type=jnp.float32,
    )
    n = lax.broadcasted_iota(jnp.int32, (nq, WIDTH), 0)
    c = lax.broadcasted_iota(jnp.int32, (nq, WIDTH), 1)
    at = ((n // 2) % NX) * nq + group * (nq // NX) + (n // (2 * NX)) * 2 + n % 2
    lines = [
        jnp.dot(
            partial,
            jnp.where(c == at + f * nall, 1.0, 0.0),
            preferred_element_type=jnp.float32,
            precision=lax.Precision.HIGHEST,
        )
        for f in range(2)
    ]
    for k, hop in enumerate((0,) + HOPS):
        pair = (group + NG - hop) % NG
        for o in range(NL):
            for v in range(NX):
                row = (k * NL + o) * 2 * NX + 2 * v
                out[v * NY + NL * pair + ((y % NL) ^ o)] = (
                    lines[0][row : row + 1, :] + lines[1][row + 1 : row + 2, :]
                )


def contract(flat, parts):
    nall = flat.shape[0] * NG
    return placed(
        contract_kernel,
        [pltpu.VMEM] * (1 + len(parts)),
        jax.ShapeDtypeStruct((nall // 2, 1, 2 * nall), jnp.float32),
        pltpu.VMEM,
        compiler_params=pltpu.CompilerParams(vmem_limit_bytes=4 << 20),
    )(flat, *parts)


def total_kernel(parts, out):
    out[...] = jnp.broadcast_to(jnp.sum(parts[...], axis=0, keepdims=True), out.shape)


def total(parts, copies):
    return placed(
        total_kernel,
        [pltpu.VMEM],
        jax.ShapeDtypeStruct((copies,) + parts.shape[1:], parts.dtype),
        pltpu.VMEM,
        compiler_params=pltpu.CompilerParams(vmem_limit_bytes=1 << 20),
    )(parts)


def finish_kernel(parts, factor, out):
    line = jnp.sum(parts[...], axis=0) * factor[...]
    n = out.shape[1]
    out[0:1, :] = line[:, :n]
    out[1:2, :] = line[:, n:]


def finish(parts, factor):
    return placed(
        finish_kernel,
        [pltpu.VMEM, pltpu.VMEM],
        jax.ShapeDtypeStruct((2, parts.shape[2] // 2), parts.dtype),
        pltpu.VMEM,
        compiler_params=pltpu.CompilerParams(vmem_limit_bytes=1 << 20),
    )(parts, factor)


def per_device(
    occ_tiles,
    vir_tiles,
    three_index,
    send_lists,
    term_pairs,
    term_tiles,
    term_count,
    z_pattern,
    laplace_point,
):
    regions = lax.axis_size("region")
    width = occ_tiles.shape[1]
    per_aux = three_index.shape[1]
    nterms = term_pairs.shape[1]
    x, y = member()

    outgoing = pick(send_lists[0], occ_tiles, vir_tiles, regions)
    recv = lax.all_to_all(outgoing, "region", 0, 0, tiled=True)

    own = lax.all_gather(three_index, "aux", axis=0, tiled=False, axis_index_groups=X_GROUPS)
    other = lax.ppermute(own, "aux", OTHER)

    def sliced(b):
        b = lax.dynamic_slice_in_dim(b, x * IB, IB, 3)
        b = lax.dynamic_slice_in_dim(b, (y % NL) * LB, LB, 4)
        b = jnp.concatenate([b[:, 0], b[:, 1]], axis=3)
        return b.reshape(NX * per_aux, IB * WIDTH)

    part = jnp.concatenate([sliced(own), sliced(other)])
    parts = [part] + [lax.ppermute(part, "aux", onward(hop)) for hop in HOPS]

    flat = transform(term_pairs[0], term_tiles[0], term_count, recv, own, other)
    partial = contract(flat, parts)

    mask_row = jnp.repeat(z_pattern[0], per_aux).astype(jnp.float32)
    weight = 0.5 + 0.125 * laplace_point[0].astype(jnp.float32)
    scale = weight / (width * jnp.sqrt(jnp.float32(regions * nterms)))
    factor = jnp.concatenate([mask_row, mask_row])[None] * scale

    spread = lax.all_to_all(partial, "aux", 0, 0, tiled=True)
    every = lax.all_to_all(total(spread, regions), "region", 0, 0, tiled=True)
    return finish(every, factor)


def solution(mesh):
    in_specs = (
        P("region", None, None),
        P("region", None, None),
        P("region", "aux", None, None),
        P("region", None, None),
        P("region", None, None),
        P("region", None, None),
        P("region"),
        P("aux", None),
        P(),
    )
    out_specs = P("aux", None)
    return jax.shard_map(
        per_device, mesh=mesh, in_specs=in_specs, out_specs=out_specs, check_vma=False
    )
```

```python
import jax
import jax.numpy as jnp
from jax import lax
from jax.experimental import pallas as pl
from jax.experimental.pallas import tpu as pltpu
from jax.sharding import PartitionSpec as P

NX = 4
NY = 8
NI = 4
NL = 2
NG = NY // NL
WIDTH = 128
IB = WIDTH // NI
LB = WIDTH // NL
KB = WIDTH // 2
X_GROUPS = [[x * NY + y for x in range(NX)] for y in range(NY)]
OTHER = [(x * NY + y, x * NY + (y ^ 1)) for x in range(NX) for y in range(NY)]
X_OTHER = [(x * NY + y, (x ^ 1) * NY + y) for x in range(NX) for y in range(NY)]
HOPS = (2, 1, NG - 1)


def onward(hop):
    return [(x * NY + y, x * NY + (y + NL * hop) % NY) for x in range(NX) for y in range(NY)]


def placed(body, ins, outs, space, **extra):
    return pl.pallas_call(
        body,
        out_shape=outs,
        in_specs=[pl.BlockSpec(memory_space=m) for m in ins],
        out_specs=pl.BlockSpec(memory_space=space),
        **extra,
    )


def member():
    aux = lax.axis_index("aux")
    return aux // NY, aux % NY


PARTS = 4


def pick_kernel(lists, occ, vir, out, rows, tiles, staged, sems):
    x, y = member()
    row = pl.multiple_of(x * IB, IB)
    col = (y % NL) * LB
    depth = pl.multiple_of((x % 2) * KB, KB)
    ntile = occ.shape[0]
    copies = [pltpu.make_async_copy(occ.at[:, pl.ds(row, IB), :], rows, sems.at[0])]
    step = ntile // PARTS
    for u in range(PARTS):
        at = pl.ds(u * step, step)
        copies.append(pltpu.make_async_copy(vir.at[at, pl.ds(depth, KB), :], tiles.at[at], sems.at[1 + u]))
    for c in copies:
        c.start()
    r = lax.broadcasted_iota(jnp.int32, (2 * WIDTH, WIDTH), 0)
    c = lax.broadcasted_iota(jnp.int32, (2 * WIDTH, WIDTH), 1)
    wanted = jnp.where(c < LB, c + col, c - LB + WIDTH + col)
    select = jnp.where(r == wanted, 1.0, 0.0).astype(jnp.bfloat16)
    for c in copies:
        c.wait()
    regions = staged.shape[0]
    step = regions // PARTS
    sent = []
    for u in range(PARTS):
        for d in range(u * step, (u + 1) * step):
            for j in range(2):
                staged[d, j * IB : (j + 1) * IB, :] = rows[lists[0, 2 * d + j]]
            pair = jnp.concatenate([tiles[lists[1, 2 * d]], tiles[lists[1, 2 * d + 1]]], axis=1)
            staged[d, 2 * IB :, :] = jnp.dot(
                pair, select, preferred_element_type=jnp.float32
            ).astype(jnp.bfloat16)
        at = pl.ds(u * step, step)
        sent.append(pltpu.make_async_copy(staged.at[at], out.at[at], sems.at[1 + PARTS + u]))
        sent[-1].start()
    for c in sent:
        c.wait()


def pick(lists, occ, vir, regions):
    smem, hbm = pltpu.SMEM, pltpu.HBM
    shape = (regions, 2 * IB + KB, WIDTH)
    return placed(
        pick_kernel,
        [smem, hbm, hbm],
        jax.ShapeDtypeStruct(shape, jnp.bfloat16),
        hbm,
        scratch_shapes=[
            pltpu.VMEM((occ.shape[0], IB, WIDTH), jnp.bfloat16),
            pltpu.VMEM((vir.shape[0], KB, WIDTH), jnp.bfloat16),
            pltpu.VMEM(shape, jnp.bfloat16),
            pltpu.SemaphoreType.DMA((1 + 2 * PARTS,)),
        ],
        compiler_params=pltpu.CompilerParams(vmem_limit_bytes=60 << 20),
        cost_estimate=pl.CostEstimate(flops=40 << 20, bytes_accessed=2 << 20, transcendentals=0),
    )(lists, occ, vir)


GROUP = 2
WIDE = 2
CHUNK = 32


def first_kernel(recv, own, other, half):
    regions = recv.shape[0]
    parity = member()[1] % NL

    def step(n, carry):
        q = n // (NX // WIDE)
        at = (n % (NX // WIDE)) * WIDE
        source = jnp.concatenate(
            [bq[at + v, q, f] for v in range(WIDE) for bq in (own, other) for f in range(2)], axis=1
        )
        for s in range(0, regions, GROUP):
            occ = recv[s : s + GROUP, 0 : 2 * IB, :].reshape(GROUP * 2 * IB, WIDTH)
            res = jnp.dot(occ, source, preferred_element_type=jnp.float32).astype(jnp.bfloat16)
            for v in range(WIDE):
                for o in range(2):
                    for f in range(2):
                        spot = ((parity ^ o) * NX + at + v) * 2 + f
                        start = pl.multiple_of(spot * IB, IB)
                        left = (v * 4 + o * 2 + f) * WIDTH
                        for u in range(2 * GROUP):
                            half[q * (2 * regions) + 2 * s + u, pl.ds(start, IB), :] = res[
                                u * IB : (u + 1) * IB, left : left + WIDTH
                            ]
        return carry

    lax.fori_loop(0, 2 * NX // WIDE, step, 0)


def first(recv, own, other):
    nq = 2 * own.shape[0] * own.shape[2]
    return placed(
        first_kernel,
        [pltpu.VMEM] * 3,
        jax.ShapeDtypeStruct((4 * recv.shape[0], nq * IB, WIDTH), jnp.bfloat16),
        pltpu.VMEM,
        compiler_params=pltpu.CompilerParams(vmem_limit_bytes=4 << 20),
        cost_estimate=pl.CostEstimate(flops=4 << 30, bytes_accessed=4 << 20, transcendentals=0),
    )(recv, own, other)


def second_kernel(pairs, tiles, count, half, kept, came, out, vir, acc, wide):
    regions = kept.shape[0]
    rows = half.shape[1]
    nq = rows // IB
    depth = pl.multiple_of((member()[0] % 2) * KB, KB)
    vir[:, pl.ds(depth, KB), :] = kept[:, 2 * IB :, :]
    vir[:, pl.ds(KB - depth, KB), :] = came[...]

    acc[...] = jnp.zeros_like(acc)
    live = count[0]
    lane = lax.broadcasted_iota(jnp.int32, (WIDTH, 2 * WIDTH), 1) // LB

    def step(n, carry):
        lhs = []
        rhs = []
        for u in range(CHUNK):
            t = n * CHUNK + u
            at = jnp.minimum(t, live - 1)
            b = tiles[at, 1]
            side = jnp.where(t < live, pairs[at, 0] * NL + b % 2, -1)
            lhs.append(half[pairs[at, 1] * (2 * regions) + tiles[at, 0]])
            tile = vir[b // 2]
            tile = jnp.concatenate([tile, tile], axis=1)
            rhs.append(jnp.where(lane == side, tile, jnp.zeros_like(tile)))
        acc[...] += jnp.dot(
            jnp.concatenate(lhs, axis=1),
            jnp.concatenate(rhs, axis=0),
            preferred_element_type=jnp.float32,
        )
        return carry

    lax.fori_loop(0, (live + CHUNK - 1) // CHUNK, step, 0)
    low = acc[:, :WIDTH]
    high = acc[:, WIDTH:]
    lanes = lax.broadcasted_iota(jnp.int32, (rows, WIDTH), 1)
    wide[...] = jnp.where(
        lanes < LB, low + pltpu.roll(low, LB, 1), high + pltpu.roll(high, LB, 1)
    )
    for i in range(IB):
        out[:, i * WIDTH : (i + 1) * WIDTH] = wide[pl.ds(i, nq, stride=IB), :].astype(jnp.bfloat16)


def second(pairs, tiles, count, half, kept, came):
    smem, vmem = pltpu.SMEM, pltpu.VMEM
    rows = half.shape[1]
    return placed(
        second_kernel,
        [smem] * 3 + [vmem] * 3,
        jax.ShapeDtypeStruct((rows // IB, IB * WIDTH), jnp.bfloat16),
        vmem,
        scratch_shapes=[
            pltpu.VMEM((kept.shape[0], WIDTH, WIDTH), jnp.bfloat16),
            pltpu.VMEM((rows, 2 * WIDTH), jnp.float32),
            pltpu.VMEM((rows, WIDTH), jnp.float32),
        ],
        compiler_params=pltpu.CompilerParams(vmem_limit_bytes=16 << 20),
        cost_estimate=pl.CostEstimate(flops=4 << 30, bytes_accessed=4 << 20, transcendentals=0),
    )(pairs, tiles, count, half, kept, came)


def contract_kernel(flat, *refs):
    parts, out = refs[:-1], refs[-1]
    y = member()[1]
    group = y // NL
    nq = flat.shape[0]
    nall = nq * NG
    partial = lax.dot_general(
        jnp.concatenate([p[...] for p in parts], axis=0),
        flat[...],
        (((1,), (1,)), ((), ())),
        preferred_element_type=jnp.float32,
    )
    n = lax.broadcasted_iota(jnp.int32, (nq, WIDTH), 0)
    c = lax.broadcasted_iota(jnp.int32, (nq, WIDTH), 1)
    at = ((n // 2) % NX) * nq + group * (nq // NX) + (n // (2 * NX)) * 2 + n % 2
    lines = [
        jnp.dot(
            partial,
            jnp.where(c == at + f * nall, 1.0, 0.0),
            preferred_element_type=jnp.float32,
            precision=lax.Precision.HIGHEST,
        )
        for f in range(2)
    ]
    for k, hop in enumerate((0,) + HOPS):
        pair = (group + NG - hop) % NG
        for o in range(NL):
            for v in range(NX):
                row = (k * NL + o) * 2 * NX + 2 * v
                out[v * NY + NL * pair + ((y % NL) ^ o)] = (
                    lines[0][row : row + 1, :] + lines[1][row + 1 : row + 2, :]
                )


def contract(flat, parts):
    nall = flat.shape[0] * NG
    return placed(
        contract_kernel,
        [pltpu.VMEM] * (1 + len(parts)),
        jax.ShapeDtypeStruct((nall // 2, 1, 2 * nall), jnp.float32),
        pltpu.VMEM,
        compiler_params=pltpu.CompilerParams(vmem_limit_bytes=4 << 20),
    )(flat, *parts)


def total_kernel(parts, out):
    out[...] = jnp.broadcast_to(jnp.sum(parts[...], axis=0, keepdims=True), out.shape)


def total(parts, copies):
    return placed(
        total_kernel,
        [pltpu.VMEM],
        jax.ShapeDtypeStruct((copies,) + parts.shape[1:], parts.dtype),
        pltpu.VMEM,
        compiler_params=pltpu.CompilerParams(vmem_limit_bytes=1 << 20),
    )(parts)


def finish_kernel(parts, factor, out):
    line = jnp.sum(parts[...], axis=0) * factor[...]
    n = out.shape[1]
    out[0:1, :] = line[:, :n]
    out[1:2, :] = line[:, n:]


def finish(parts, factor):
    return placed(
        finish_kernel,
        [pltpu.VMEM, pltpu.VMEM],
        jax.ShapeDtypeStruct((2, parts.shape[2] // 2), parts.dtype),
        pltpu.VMEM,
        compiler_params=pltpu.CompilerParams(vmem_limit_bytes=1 << 20),
    )(parts, factor)


def per_device(
    occ_tiles,
    vir_tiles,
    three_index,
    send_lists,
    term_pairs,
    term_tiles,
    term_count,
    z_pattern,
    laplace_point,
):
    regions = lax.axis_size("region")
    width = occ_tiles.shape[1]
    per_aux = three_index.shape[1]
    nterms = term_pairs.shape[1]
    x, y = member()

    outgoing = pick(send_lists[0], occ_tiles, vir_tiles, regions)
    recv = lax.all_to_all(outgoing, "region", 0, 0, tiled=True)

    own = lax.all_gather(three_index, "aux", axis=0, tiled=False, axis_index_groups=X_GROUPS)
    def sliced(b, side):
        b = lax.dynamic_slice_in_dim(b, x * IB, IB, 3)
        b = lax.dynamic_slice_in_dim(b, side * LB, LB, 4)
        b = jnp.concatenate([b[:, 0], b[:, 1]], axis=3)
        return b.reshape(NX * per_aux, IB * WIDTH)

    theirs = lax.ppermute(sliced(own, 1 - y % NL), "aux", OTHER)
    late, theirs = lax.optimization_barrier((own, theirs))
    other = lax.ppermute(late, "aux", OTHER)
    part = jnp.concatenate([sliced(own, y % NL), theirs])
    parts = [part] + [lax.ppermute(part, "aux", onward(hop)) for hop in HOPS]

    mask_row = jnp.repeat(z_pattern[0], per_aux).astype(jnp.float32)
    weight = 0.5 + 0.125 * laplace_point[0].astype(jnp.float32)
    scale = weight / (width * jnp.sqrt(jnp.float32(regions * nterms)))
    factor = jnp.concatenate([mask_row, mask_row])[None] * scale

    came = lax.ppermute(recv[:, 2 * IB :, :], "aux", X_OTHER)
    half = first(recv, own, other)
    half, factor = lax.optimization_barrier((half, factor))
    flat = second(term_pairs[0], term_tiles[0], term_count, half, recv, came)
    partial = contract(flat, parts)

    spread = lax.all_to_all(partial, "aux", 0, 0, tiled=True)
    every = lax.all_to_all(total(spread, regions), "region", 0, 0, tiled=True)
    return finish(every, factor)


def solution(mesh):
    in_specs = (
        P("region", None, None),
        P("region", None, None),
        P("region", "aux", None, None),
        P("region", None, None),
        P("region", None, None),
        P("region", None, None),
        P("region"),
        P("aux", None),
        P(),
    )
    out_specs = P("aux", None)
    return jax.shard_map(
        per_device, mesh=mesh, in_specs=in_specs, out_specs=out_specs, check_vma=False
    )
```

```python
import jax
import jax.numpy as jnp
from jax import lax
from jax.experimental import pallas as pl
from jax.experimental.pallas import tpu as pltpu
from jax.sharding import PartitionSpec as P

NX = 4
NY = 8
NI = 4
NL = 2
NG = NY // NL
WIDTH = 128
IB = WIDTH // NI
LB = WIDTH // NL
KB = WIDTH // 2
X_GROUPS = [[x * NY + y for x in range(NX)] for y in range(NY)]
OTHER = [(x * NY + y, x * NY + (y ^ 1)) for x in range(NX) for y in range(NY)]
X_OTHER = [(x * NY + y, (x ^ 1) * NY + y) for x in range(NX) for y in range(NY)]
Y_GROUPS = [[x * NY + y for y in range(NY)] for x in range(NX)]


def placed(body, ins, outs, space, **extra):
    return pl.pallas_call(
        body,
        out_shape=outs,
        in_specs=[pl.BlockSpec(memory_space=m) for m in ins],
        out_specs=pl.BlockSpec(memory_space=space),
        **extra,
    )


def member():
    aux = lax.axis_index("aux")
    return aux // NY, aux % NY


PARTS = 4


def pick_kernel(lists, occ, vir, out, rows, tiles, staged, sems):
    x, y = member()
    row = pl.multiple_of(x * IB, IB)
    col = (y % NL) * LB
    depth = pl.multiple_of((x % 2) * KB, KB)
    ntile = occ.shape[0]
    copies = [pltpu.make_async_copy(occ.at[:, pl.ds(row, IB), :], rows, sems.at[0])]
    step = ntile // PARTS
    for u in range(PARTS):
        at = pl.ds(u * step, step)
        copies.append(pltpu.make_async_copy(vir.at[at, pl.ds(depth, KB), :], tiles.at[at], sems.at[1 + u]))
    for c in copies:
        c.start()
    r = lax.broadcasted_iota(jnp.int32, (2 * WIDTH, WIDTH), 0)
    c = lax.broadcasted_iota(jnp.int32, (2 * WIDTH, WIDTH), 1)
    wanted = jnp.where(c < LB, c + col, c - LB + WIDTH + col)
    select = jnp.where(r == wanted, 1.0, 0.0).astype(jnp.bfloat16)
    for c in copies:
        c.wait()
    regions = staged.shape[0]
    step = regions // PARTS
    sent = []
    for u in range(PARTS):
        for d in range(u * step, (u + 1) * step):
            for j in range(2):
                staged[d, j * IB : (j + 1) * IB, :] = rows[lists[0, 2 * d + j]]
            pair = jnp.concatenate([tiles[lists[1, 2 * d]], tiles[lists[1, 2 * d + 1]]], axis=1)
            staged[d, 2 * IB :, :] = jnp.dot(
                pair, select, preferred_element_type=jnp.float32
            ).astype(jnp.bfloat16)
        at = pl.ds(u * step, step)
        sent.append(pltpu.make_async_copy(staged.at[at], out.at[at], sems.at[1 + PARTS + u]))
        sent[-1].start()
    for c in sent:
        c.wait()


def pick(lists, occ, vir, regions):
    smem, hbm = pltpu.SMEM, pltpu.HBM
    shape = (regions, 2 * IB + KB, WIDTH)
    return placed(
        pick_kernel,
        [smem, hbm, hbm],
        jax.ShapeDtypeStruct(shape, jnp.bfloat16),
        hbm,
        scratch_shapes=[
            pltpu.VMEM((occ.shape[0], IB, WIDTH), jnp.bfloat16),
            pltpu.VMEM((vir.shape[0], KB, WIDTH), jnp.bfloat16),
            pltpu.VMEM(shape, jnp.bfloat16),
            pltpu.SemaphoreType.DMA((1 + 2 * PARTS,)),
        ],
        compiler_params=pltpu.CompilerParams(vmem_limit_bytes=60 << 20),
        cost_estimate=pl.CostEstimate(flops=40 << 20, bytes_accessed=2 << 20, transcendentals=0),
    )(lists, occ, vir)


GROUP = 2
WIDE = 2
CHUNK = 32


def first_kernel(recv, own, other, half):
    regions = recv.shape[0]
    parity = member()[1] % NL

    def step(n, carry):
        q = n // (NX // WIDE)
        at = (n % (NX // WIDE)) * WIDE
        source = jnp.concatenate(
            [bq[at + v, q, f] for v in range(WIDE) for bq in (own, other) for f in range(2)], axis=1
        )
        for s in range(0, regions, GROUP):
            occ = recv[s : s + GROUP, 0 : 2 * IB, :].reshape(GROUP * 2 * IB, WIDTH)
            res = jnp.dot(occ, source, preferred_element_type=jnp.float32).astype(jnp.bfloat16)
            for v in range(WIDE):
                for o in range(2):
                    for f in range(2):
                        spot = ((parity ^ o) * NX + at + v) * 2 + f
                        start = pl.multiple_of(spot * IB, IB)
                        left = (v * 4 + o * 2 + f) * WIDTH
                        for u in range(2 * GROUP):
                            half[q * (2 * regions) + 2 * s + u, pl.ds(start, IB), :] = res[
                                u * IB : (u + 1) * IB, left : left + WIDTH
                            ]
        return carry

    lax.fori_loop(0, 2 * NX // WIDE, step, 0)


def first(recv, own, other):
    nq = 2 * own.shape[0] * own.shape[2]
    return placed(
        first_kernel,
        [pltpu.VMEM] * 3,
        jax.ShapeDtypeStruct((4 * recv.shape[0], nq * IB, WIDTH), jnp.bfloat16),
        pltpu.VMEM,
        compiler_params=pltpu.CompilerParams(vmem_limit_bytes=4 << 20),
        cost_estimate=pl.CostEstimate(flops=4 << 30, bytes_accessed=4 << 20, transcendentals=0),
    )(recv, own, other)


def second_kernel(pairs, tiles, count, half, kept, came, out, vir, acc, wide):
    regions = kept.shape[0]
    rows = half.shape[1]
    nq = rows // IB
    depth = pl.multiple_of((member()[0] % 2) * KB, KB)
    vir[:, pl.ds(depth, KB), :] = kept[:, 2 * IB :, :]
    vir[:, pl.ds(KB - depth, KB), :] = came[...]

    acc[...] = jnp.zeros_like(acc)
    live = count[0]
    lane = lax.broadcasted_iota(jnp.int32, (WIDTH, 2 * WIDTH), 1) // LB

    def step(n, carry):
        lhs = []
        rhs = []
        for u in range(CHUNK):
            t = n * CHUNK + u
            at = jnp.minimum(t, live - 1)
            b = tiles[at, 1]
            side = jnp.where(t < live, pairs[at, 0] * NL + b % 2, -1)
            lhs.append(half[pairs[at, 1] * (2 * regions) + tiles[at, 0]])
            tile = vir[b // 2]
            tile = jnp.concatenate([tile, tile], axis=1)
            rhs.append(jnp.where(lane == side, tile, jnp.zeros_like(tile)))
        acc[...] += jnp.dot(
            jnp.concatenate(lhs, axis=1),
            jnp.concatenate(rhs, axis=0),
            preferred_element_type=jnp.float32,
        )
        return carry

    lax.fori_loop(0, (live + CHUNK - 1) // CHUNK, step, 0)
    low = acc[:, :WIDTH]
    high = acc[:, WIDTH:]
    lanes = lax.broadcasted_iota(jnp.int32, (rows, WIDTH), 1)
    wide[...] = jnp.where(
        lanes < LB, low + pltpu.roll(low, LB, 1), high + pltpu.roll(high, LB, 1)
    )
    for i in range(IB):
        out[:, i * WIDTH : (i + 1) * WIDTH] = wide[pl.ds(i, nq, stride=IB), :].astype(jnp.bfloat16)


def second(pairs, tiles, count, half, kept, came):
    smem, vmem = pltpu.SMEM, pltpu.VMEM
    rows = half.shape[1]
    return placed(
        second_kernel,
        [smem] * 3 + [vmem] * 3,
        jax.ShapeDtypeStruct((rows // IB, IB * WIDTH), jnp.bfloat16),
        vmem,
        scratch_shapes=[
            pltpu.VMEM((kept.shape[0], WIDTH, WIDTH), jnp.bfloat16),
            pltpu.VMEM((rows, 2 * WIDTH), jnp.float32),
            pltpu.VMEM((rows, WIDTH), jnp.float32),
        ],
        compiler_params=pltpu.CompilerParams(vmem_limit_bytes=16 << 20),
        cost_estimate=pl.CostEstimate(flops=4 << 30, bytes_accessed=4 << 20, transcendentals=0),
    )(pairs, tiles, count, half, kept, came)


def contract_kernel(flat, bp, out):
    y = member()[1]
    nq = flat.shape[0]
    nall = nq * NG
    partial = lax.dot_general(
        bp[...], flat[...], (((1,), (1,)), ((), ())), preferred_element_type=jnp.float32
    )
    n = lax.broadcasted_iota(jnp.int32, (nq, WIDTH), 0)
    c = lax.broadcasted_iota(jnp.int32, (nq, WIDTH), 1)
    at = ((n // 2) % NX) * nq + (y // NL) * (nq // NX) + (n // (2 * NX)) * 2 + n % 2
    lines = [
        jnp.dot(
            partial,
            jnp.where(c == at + f * nall, 1.0, 0.0),
            preferred_element_type=jnp.float32,
            precision=lax.Precision.HIGHEST,
        )
        for f in range(2)
    ]
    for v in range(NX):
        for w in range(NY):
            row = 2 * (w * NX + v)
            out[v * NY + w] = lines[0][row : row + 1, :] + lines[1][row + 1 : row + 2, :]


def contract(flat, bp):
    nall = flat.shape[0] * NG
    return placed(
        contract_kernel,
        [pltpu.VMEM] * 2,
        jax.ShapeDtypeStruct((nall // 2, 1, 2 * nall), jnp.float32),
        pltpu.VMEM,
        compiler_params=pltpu.CompilerParams(vmem_limit_bytes=4 << 20),
    )(flat, bp)


def total_kernel(parts, out):
    out[...] = jnp.broadcast_to(jnp.sum(parts[...], axis=0, keepdims=True), out.shape)


def total(parts, copies):
    return placed(
        total_kernel,
        [pltpu.VMEM],
        jax.ShapeDtypeStruct((copies,) + parts.shape[1:], parts.dtype),
        pltpu.VMEM,
        compiler_params=pltpu.CompilerParams(vmem_limit_bytes=1 << 20),
    )(parts)


def finish_kernel(parts, factor, out):
    line = jnp.sum(parts[...], axis=0) * factor[...]
    n = out.shape[1]
    out[0:1, :] = line[:, :n]
    out[1:2, :] = line[:, n:]


def finish(parts, factor):
    return placed(
        finish_kernel,
        [pltpu.VMEM, pltpu.VMEM],
        jax.ShapeDtypeStruct((2, parts.shape[2] // 2), parts.dtype),
        pltpu.VMEM,
        compiler_params=pltpu.CompilerParams(vmem_limit_bytes=1 << 20),
    )(parts, factor)


def per_device(
    occ_tiles,
    vir_tiles,
    three_index,
    send_lists,
    term_pairs,
    term_tiles,
    term_count,
    z_pattern,
    laplace_point,
):
    regions = lax.axis_size("region")
    width = occ_tiles.shape[1]
    per_aux = three_index.shape[1]
    nterms = term_pairs.shape[1]
    x = member()[0]

    outgoing = pick(send_lists[0], occ_tiles, vir_tiles, regions)

    outgoing, mine = lax.optimization_barrier((outgoing, three_index))
    recv = lax.all_to_all(outgoing, "region", 0, 0, tiled=True)
    own = lax.all_gather(mine, "aux", axis=0, tiled=False, axis_index_groups=X_GROUPS)

    part = lax.dynamic_slice_in_dim(own, x * IB, IB, 3)
    cut = [
        jnp.concatenate([part[:, 0, :, :, c : c + LB], part[:, 1, :, :, c : c + LB]], axis=3)
        for c in range(0, width, LB)
    ]
    cut = jnp.stack(cut).reshape(NL, NX * per_aux, IB * WIDTH)
    sent = jnp.concatenate([cut] * (NY // NL))
    bp = lax.all_to_all(sent, "aux", 0, 0, tiled=True, axis_index_groups=Y_GROUPS)
    bp = bp.reshape(NY * NX * per_aux, IB * WIDTH)
    other = lax.ppermute(own, "aux", OTHER)

    mask_row = jnp.repeat(z_pattern[0], per_aux).astype(jnp.float32)
    weight = 0.5 + 0.125 * laplace_point[0].astype(jnp.float32)
    scale = weight / (width * jnp.sqrt(jnp.float32(regions * nterms)))
    factor = jnp.concatenate([mask_row, mask_row])[None] * scale

    came = lax.ppermute(recv[:, 2 * IB :, :], "aux", X_OTHER)
    half = first(recv, own, other)
    half, factor = lax.optimization_barrier((half, factor))
    flat = second(term_pairs[0], term_tiles[0], term_count, half, recv, came)
    partial = contract(flat, bp)

    spread = lax.all_to_all(partial, "aux", 0, 0, tiled=True)
    every = lax.all_to_all(total(spread, regions), "region", 0, 0, tiled=True)
    return finish(every, factor)


def solution(mesh):
    in_specs = (
        P("region", None, None),
        P("region", None, None),
        P("region", "aux", None, None),
        P("region", None, None),
        P("region", None, None),
        P("region", None, None),
        P("region"),
        P("aux", None),
        P(),
    )
    out_specs = P("aux", None)
    return jax.shard_map(
        per_device, mesh=mesh, in_specs=in_specs, out_specs=out_specs, check_vma=False
    )
```

```python
import jax
import jax.numpy as jnp
from jax import lax
from jax.experimental import pallas as pl
from jax.experimental.pallas import tpu as pltpu
from jax.sharding import PartitionSpec as P

NX = 4
NY = 8
NI = 4
NL = 2
NG = NY // NL
WIDTH = 128
IB = WIDTH // NI
LB = WIDTH // NL
KB = WIDTH // 2
X_GROUPS = [[x * NY + y for x in range(NX)] for y in range(NY)]
OTHER = [(x * NY + y, x * NY + (y ^ 1)) for x in range(NX) for y in range(NY)]
X_OTHER = [(x * NY + y, (x ^ 1) * NY + y) for x in range(NX) for y in range(NY)]
HOPS = (2, 1, NG - 1)


def onward(hop):
    return [(x * NY + y, x * NY + (y + NL * hop) % NY) for x in range(NX) for y in range(NY)]


def placed(body, ins, outs, space, **extra):
    return pl.pallas_call(
        body,
        out_shape=outs,
        in_specs=[pl.BlockSpec(memory_space=m) for m in ins],
        out_specs=pl.BlockSpec(memory_space=space),
        **extra,
    )


def member():
    aux = lax.axis_index("aux")
    return aux // NY, aux % NY


PARTS = 4


def pick_kernel(lists, occ, vir, out, rows, tiles, staged, sems):
    x, y = member()
    row = pl.multiple_of(x * IB, IB)
    col = (y % NL) * LB
    depth = pl.multiple_of((x % 2) * KB, KB)
    ntile = occ.shape[0]
    copies = [pltpu.make_async_copy(occ.at[:, pl.ds(row, IB), :], rows, sems.at[0])]
    step = ntile // PARTS
    for u in range(PARTS):
        at = pl.ds(u * step, step)
        copies.append(pltpu.make_async_copy(vir.at[at, pl.ds(depth, KB), :], tiles.at[at], sems.at[1 + u]))
    for c in copies:
        c.start()
    r = lax.broadcasted_iota(jnp.int32, (2 * WIDTH, WIDTH), 0)
    c = lax.broadcasted_iota(jnp.int32, (2 * WIDTH, WIDTH), 1)
    wanted = jnp.where(c < LB, c + col, c - LB + WIDTH + col)
    select = jnp.where(r == wanted, 1.0, 0.0).astype(jnp.bfloat16)
    for c in copies:
        c.wait()
    regions = staged.shape[0]
    step = regions // PARTS
    sent = []
    for u in range(PARTS):
        for d in range(u * step, (u + 1) * step):
            for j in range(2):
                staged[d, j * IB : (j + 1) * IB, :] = rows[lists[0, 2 * d + j]]
            pair = jnp.concatenate([tiles[lists[1, 2 * d]], tiles[lists[1, 2 * d + 1]]], axis=1)
            staged[d, 2 * IB :, :] = jnp.dot(
                pair, select, preferred_element_type=jnp.float32
            ).astype(jnp.bfloat16)
        at = pl.ds(u * step, step)
        sent.append(pltpu.make_async_copy(staged.at[at], out.at[at], sems.at[1 + PARTS + u]))
        sent[-1].start()
    for c in sent:
        c.wait()


def pick(lists, occ, vir, regions):
    smem, hbm = pltpu.SMEM, pltpu.HBM
    shape = (regions, 2 * IB + KB, WIDTH)
    return placed(
        pick_kernel,
        [smem, hbm, hbm],
        jax.ShapeDtypeStruct(shape, jnp.bfloat16),
        hbm,
        scratch_shapes=[
            pltpu.VMEM((occ.shape[0], IB, WIDTH), jnp.bfloat16),
            pltpu.VMEM((vir.shape[0], KB, WIDTH), jnp.bfloat16),
            pltpu.VMEM(shape, jnp.bfloat16),
            pltpu.SemaphoreType.DMA((1 + 2 * PARTS,)),
        ],
        compiler_params=pltpu.CompilerParams(vmem_limit_bytes=60 << 20),
        cost_estimate=pl.CostEstimate(flops=40 << 20, bytes_accessed=2 << 20, transcendentals=0),
    )(lists, occ, vir)


GROUP = 2
WIDE = 2
CHUNK = 32


def first_kernel(recv, own, other, half):
    regions = recv.shape[0]
    parity = member()[1] % NL

    def step(n, carry):
        q = n // (NX // WIDE)
        at = (n % (NX // WIDE)) * WIDE
        source = jnp.concatenate(
            [bq[at + v, q, f] for v in range(WIDE) for bq in (own, other) for f in range(2)], axis=1
        )
        for s in range(0, regions, GROUP):
            occ = recv[s : s + GROUP, 0 : 2 * IB, :].reshape(GROUP * 2 * IB, WIDTH)
            res = jnp.dot(occ, source, preferred_element_type=jnp.float32).astype(jnp.bfloat16)
            for v in range(WIDE):
                for o in range(2):
                    for f in range(2):
                        spot = ((parity ^ o) * NX + at + v) * 2 + f
                        start = pl.multiple_of(spot * IB, IB)
                        left = (v * 4 + o * 2 + f) * WIDTH
                        for u in range(2 * GROUP):
                            half[q * (2 * regions) + 2 * s + u, pl.ds(start, IB), :] = res[
                                u * IB : (u + 1) * IB, left : left + WIDTH
                            ]
        return carry

    lax.fori_loop(0, 2 * NX // WIDE, step, 0)


def first(recv, own, other):
    nq = 2 * own.shape[0] * own.shape[2]
    return placed(
        first_kernel,
        [pltpu.VMEM] * 3,
        jax.ShapeDtypeStruct((4 * recv.shape[0], nq * IB, WIDTH), jnp.bfloat16),
        pltpu.VMEM,
        compiler_params=pltpu.CompilerParams(vmem_limit_bytes=4 << 20),
        cost_estimate=pl.CostEstimate(flops=4 << 30, bytes_accessed=4 << 20, transcendentals=0),
    )(recv, own, other)


def second_kernel(pairs, tiles, count, half, kept, came, out, vir, acc, wide):
    regions = kept.shape[0]
    rows = half.shape[1]
    nq = rows // IB
    depth = pl.multiple_of((member()[0] % 2) * KB, KB)
    vir[:, pl.ds(depth, KB), :] = kept[:, 2 * IB :, :]
    vir[:, pl.ds(KB - depth, KB), :] = came[...]

    acc[...] = jnp.zeros_like(acc)
    live = count[0]
    lane = lax.broadcasted_iota(jnp.int32, (WIDTH, 2 * WIDTH), 1) // LB

    def step(n, carry):
        lhs = []
        rhs = []
        for u in range(CHUNK):
            t = n * CHUNK + u
            at = jnp.minimum(t, live - 1)
            b = tiles[at, 1]
            side = jnp.where(t < live, pairs[at, 0] * NL + b % 2, -1)
            lhs.append(half[pairs[at, 1] * (2 * regions) + tiles[at, 0]])
            tile = vir[b // 2]
            tile = jnp.concatenate([tile, tile], axis=1)
            rhs.append(jnp.where(lane == side, tile, jnp.zeros_like(tile)))
        acc[...] += jnp.dot(
            jnp.concatenate(lhs, axis=1),
            jnp.concatenate(rhs, axis=0),
            preferred_element_type=jnp.float32,
        )
        return carry

    lax.fori_loop(0, (live + CHUNK - 1) // CHUNK, step, 0)
    low = acc[:, :WIDTH]
    high = acc[:, WIDTH:]
    lanes = lax.broadcasted_iota(jnp.int32, (rows, WIDTH), 1)
    wide[...] = jnp.where(
        lanes < LB, low + pltpu.roll(low, LB, 1), high + pltpu.roll(high, LB, 1)
    )
    for i in range(IB):
        out[:, i * WIDTH : (i + 1) * WIDTH] = wide[pl.ds(i, nq, stride=IB), :].astype(jnp.bfloat16)


def second(pairs, tiles, count, half, kept, came):
    smem, vmem = pltpu.SMEM, pltpu.VMEM
    rows = half.shape[1]
    return placed(
        second_kernel,
        [smem] * 3 + [vmem] * 3,
        jax.ShapeDtypeStruct((rows // IB, IB * WIDTH), jnp.bfloat16),
        vmem,
        scratch_shapes=[
            pltpu.VMEM((kept.shape[0], WIDTH, WIDTH), jnp.bfloat16),
            pltpu.VMEM((rows, 2 * WIDTH), jnp.float32),
            pltpu.VMEM((rows, WIDTH), jnp.float32),
        ],
        compiler_params=pltpu.CompilerParams(vmem_limit_bytes=16 << 20),
        cost_estimate=pl.CostEstimate(flops=4 << 30, bytes_accessed=4 << 20, transcendentals=0),
    )(pairs, tiles, count, half, kept, came)


def contract_kernel(flat, *refs):
    parts, out = refs[:-1], refs[-1]
    y = member()[1]
    group = y // NL
    nq = flat.shape[0]
    nall = nq * NG
    partial = lax.dot_general(
        jnp.concatenate([p[...] for p in parts], axis=0),
        flat[...],
        (((1,), (1,)), ((), ())),
        preferred_element_type=jnp.float32,
    )
    n = lax.broadcasted_iota(jnp.int32, (nq, WIDTH), 0)
    c = lax.broadcasted_iota(jnp.int32, (nq, WIDTH), 1)
    at = ((n // 2) % NX) * nq + group * (nq // NX) + (n // (2 * NX)) * 2 + n % 2
    lines = [
        jnp.dot(
            partial,
            jnp.where(c == at + f * nall, 1.0, 0.0),
            preferred_element_type=jnp.float32,
            precision=lax.Precision.HIGHEST,
        )
        for f in range(2)
    ]
    for k, hop in enumerate((0,) + HOPS):
        pair = (group + NG - hop) % NG
        for o in range(NL):
            for v in range(NX):
                row = (k * NL + o) * 2 * NX + 2 * v
                out[v * NY + NL * pair + ((y % NL) ^ o)] = (
                    lines[0][row : row + 1, :] + lines[1][row + 1 : row + 2, :]
                )


def contract(flat, parts):
    nall = flat.shape[0] * NG
    return placed(
        contract_kernel,
        [pltpu.VMEM] * (1 + len(parts)),
        jax.ShapeDtypeStruct((nall // 2, 1, 2 * nall), jnp.float32),
        pltpu.VMEM,
        compiler_params=pltpu.CompilerParams(vmem_limit_bytes=4 << 20),
    )(flat, *parts)


def total_kernel(parts, out):
    out[...] = jnp.broadcast_to(jnp.sum(parts[...], axis=0, keepdims=True), out.shape)


def total(parts, copies):
    return placed(
        total_kernel,
        [pltpu.VMEM],
        jax.ShapeDtypeStruct((copies,) + parts.shape[1:], parts.dtype),
        pltpu.VMEM,
        compiler_params=pltpu.CompilerParams(vmem_limit_bytes=1 << 20),
    )(parts)


def finish_kernel(parts, factor, out):
    line = jnp.sum(parts[...], axis=0) * factor[...]
    n = out.shape[1]
    out[0:1, :] = line[:, :n]
    out[1:2, :] = line[:, n:]


def finish(parts, factor):
    return placed(
        finish_kernel,
        [pltpu.VMEM, pltpu.VMEM],
        jax.ShapeDtypeStruct((2, parts.shape[2] // 2), parts.dtype),
        pltpu.VMEM,
        compiler_params=pltpu.CompilerParams(vmem_limit_bytes=1 << 20),
    )(parts, factor)


def per_device(
    occ_tiles,
    vir_tiles,
    three_index,
    send_lists,
    term_pairs,
    term_tiles,
    term_count,
    z_pattern,
    laplace_point,
):
    regions = lax.axis_size("region")
    width = occ_tiles.shape[1]
    per_aux = three_index.shape[1]
    nterms = term_pairs.shape[1]
    x, y = member()

    outgoing = pick(send_lists[0], occ_tiles, vir_tiles, regions)
    recv = lax.all_to_all(outgoing, "region", 0, 0, tiled=True)

    own = lax.all_gather(three_index, "aux", axis=0, tiled=False, axis_index_groups=X_GROUPS)
    def sliced(b, side):
        b = lax.dynamic_slice_in_dim(b, x * IB, IB, 3)
        b = lax.dynamic_slice_in_dim(b, side * LB, LB, 4)
        b = jnp.concatenate([b[:, 0], b[:, 1]], axis=3)
        return b.reshape(NX * per_aux, IB * WIDTH)

    theirs = lax.ppermute(sliced(own, 1 - y % NL), "aux", OTHER)
    late, theirs = lax.optimization_barrier((own, theirs))
    other = lax.ppermute(late, "aux", OTHER)
    part = jnp.concatenate([sliced(own, y % NL), theirs])
    parts = [part] + [lax.ppermute(part, "aux", onward(hop)) for hop in HOPS[:2]]

    mask_row = jnp.repeat(z_pattern[0], per_aux).astype(jnp.float32)
    weight = 0.5 + 0.125 * laplace_point[0].astype(jnp.float32)
    scale = weight / (width * jnp.sqrt(jnp.float32(regions * nterms)))
    factor = jnp.concatenate([mask_row, mask_row])[None] * scale

    came = lax.ppermute(recv[:, 2 * IB :, :], "aux", X_OTHER)
    half = first(recv, own, other)
    half, factor, late = lax.optimization_barrier((half, factor, part))
    parts.append(lax.ppermute(late, "aux", onward(HOPS[2])))
    flat = second(term_pairs[0], term_tiles[0], term_count, half, recv, came)
    partial = contract(flat, parts)

    spread = lax.all_to_all(partial, "aux", 0, 0, tiled=True)
    every = lax.all_to_all(total(spread, regions), "region", 0, 0, tiled=True)
    return finish(every, factor)


def solution(mesh):
    in_specs = (
        P("region", None, None),
        P("region", None, None),
        P("region", "aux", None, None),
        P("region", None, None),
        P("region", None, None),
        P("region", None, None),
        P("region"),
        P("aux", None),
        P(),
    )
    out_specs = P("aux", None)
    return jax.shard_map(
        per_device, mesh=mesh, in_specs=in_specs, out_specs=out_specs, check_vma=False
    )
```

```python
import jax
import jax.numpy as jnp
from jax import lax
from jax.experimental import pallas as pl
from jax.experimental.pallas import tpu as pltpu
from jax.sharding import PartitionSpec as P

NX = 4
NY = 8
NI = 4
NL = 2
NG = NY // NL
WIDTH = 128
IB = WIDTH // NI
LB = WIDTH // NL
KB = WIDTH // 2
X_GROUPS = [[x * NY + y for x in range(NX)] for y in range(NY)]
OTHER = [(x * NY + y, x * NY + (y ^ 1)) for x in range(NX) for y in range(NY)]
X_OTHER = [(x * NY + y, (x ^ 1) * NY + y) for x in range(NX) for y in range(NY)]
HOPS = (2, 1, NG - 1)


def onward(hop):
    return [(x * NY + y, x * NY + (y + NL * hop) % NY) for x in range(NX) for y in range(NY)]


def placed(body, ins, outs, space, **extra):
    return pl.pallas_call(
        body,
        out_shape=outs,
        in_specs=[pl.BlockSpec(memory_space=m) for m in ins],
        out_specs=pl.BlockSpec(memory_space=space),
        **extra,
    )


def member():
    aux = lax.axis_index("aux")
    return aux // NY, aux % NY


PARTS = 4


def pick_kernel(lists, occ, vir, out, rows, tiles, staged, sems):
    x, y = member()
    row = pl.multiple_of(x * IB, IB)
    col = (y % NL) * LB
    depth = pl.multiple_of((x % 2) * KB, KB)
    ntile = occ.shape[0]
    copies = [pltpu.make_async_copy(occ.at[:, pl.ds(row, IB), :], rows, sems.at[0])]
    step = ntile // PARTS
    for u in range(PARTS):
        at = pl.ds(u * step, step)
        copies.append(pltpu.make_async_copy(vir.at[at, pl.ds(depth, KB), :], tiles.at[at], sems.at[1 + u]))
    for c in copies:
        c.start()
    r = lax.broadcasted_iota(jnp.int32, (2 * WIDTH, WIDTH), 0)
    c = lax.broadcasted_iota(jnp.int32, (2 * WIDTH, WIDTH), 1)
    wanted = jnp.where(c < LB, c + col, c - LB + WIDTH + col)
    select = jnp.where(r == wanted, 1.0, 0.0).astype(jnp.bfloat16)
    for c in copies:
        c.wait()
    regions = staged.shape[0]
    step = regions // PARTS
    sent = []
    for u in range(PARTS):
        for d in range(u * step, (u + 1) * step):
            for j in range(2):
                staged[d, j * IB : (j + 1) * IB, :] = rows[lists[0, 2 * d + j]]
            pair = jnp.concatenate([tiles[lists[1, 2 * d]], tiles[lists[1, 2 * d + 1]]], axis=1)
            staged[d, 2 * IB :, :] = jnp.dot(
                pair, select, preferred_element_type=jnp.float32
            ).astype(jnp.bfloat16)
        at = pl.ds(u * step, step)
        sent.append(pltpu.make_async_copy(staged.at[at], out.at[at], sems.at[1 + PARTS + u]))
        sent[-1].start()
    for c in sent:
        c.wait()


def pick(lists, occ, vir, regions):
    smem, hbm = pltpu.SMEM, pltpu.HBM
    shape = (regions, 2 * IB + KB, WIDTH)
    return placed(
        pick_kernel,
        [smem, hbm, hbm],
        jax.ShapeDtypeStruct(shape, jnp.bfloat16),
        hbm,
        scratch_shapes=[
            pltpu.VMEM((occ.shape[0], IB, WIDTH), jnp.bfloat16),
            pltpu.VMEM((vir.shape[0], KB, WIDTH), jnp.bfloat16),
            pltpu.VMEM(shape, jnp.bfloat16),
            pltpu.SemaphoreType.DMA((1 + 2 * PARTS,)),
        ],
        compiler_params=pltpu.CompilerParams(vmem_limit_bytes=60 << 20),
        cost_estimate=pl.CostEstimate(flops=40 << 20, bytes_accessed=2 << 20, transcendentals=0),
    )(lists, occ, vir)


GROUP = 2
WIDE = 2
CHUNK = 32


def first_kernel(recv, own, other, half):
    regions = recv.shape[0]
    parity = member()[1] % NL

    def step(n, carry):
        q = n // (NX // WIDE)
        at = (n % (NX // WIDE)) * WIDE
        source = jnp.concatenate(
            [bq[at + v, q, f] for v in range(WIDE) for bq in (own, other) for f in range(2)], axis=1
        )
        for s in range(0, regions, GROUP):
            occ = recv[s : s + GROUP, 0 : 2 * IB, :].reshape(GROUP * 2 * IB, WIDTH)
            res = jnp.dot(occ, source, preferred_element_type=jnp.float32).astype(jnp.bfloat16)
            for v in range(WIDE):
                for o in range(2):
                    for f in range(2):
                        spot = ((parity ^ o) * NX + at + v) * 2 + f
                        start = pl.multiple_of(spot * IB, IB)
                        left = (v * 4 + o * 2 + f) * WIDTH
                        for u in range(2 * GROUP):
                            half[q * (2 * regions) + 2 * s + u, pl.ds(start, IB), :] = res[
                                u * IB : (u + 1) * IB, left : left + WIDTH
                            ]
        return carry

    lax.fori_loop(0, 2 * NX // WIDE, step, 0)


def first(recv, own, other):
    nq = 2 * own.shape[0] * own.shape[2]
    return placed(
        first_kernel,
        [pltpu.VMEM] * 3,
        jax.ShapeDtypeStruct((4 * recv.shape[0], nq * IB, WIDTH), jnp.bfloat16),
        pltpu.VMEM,
        compiler_params=pltpu.CompilerParams(vmem_limit_bytes=4 << 20),
        cost_estimate=pl.CostEstimate(flops=4 << 30, bytes_accessed=4 << 20, transcendentals=0),
    )(recv, own, other)


def second_kernel(pairs, tiles, count, half, kept, came, out, vir, acc, wide):
    regions = kept.shape[0]
    rows = half.shape[1]
    nq = rows // IB
    depth = pl.multiple_of((member()[0] % 2) * KB, KB)
    vir[:, pl.ds(depth, KB), :] = kept[:, 2 * IB :, :]
    vir[:, pl.ds(KB - depth, KB), :] = came[...]

    acc[...] = jnp.zeros_like(acc)
    live = count[0]
    lane = lax.broadcasted_iota(jnp.int32, (WIDTH, 2 * WIDTH), 1) // LB

    def step(n, carry):
        lhs = []
        rhs = []
        for u in range(CHUNK):
            t = n * CHUNK + u
            at = jnp.minimum(t, live - 1)
            b = tiles[1, at]
            side = jnp.where(t < live, pairs[0, at] * NL + b % 2, -1)
            lhs.append(half[pairs[1, at] * (2 * regions) + tiles[0, at]])
            tile = vir[b // 2]
            tile = jnp.concatenate([tile, tile], axis=1)
            rhs.append(jnp.where(lane == side, tile, jnp.zeros_like(tile)))
        acc[...] += jnp.dot(
            jnp.concatenate(lhs, axis=1),
            jnp.concatenate(rhs, axis=0),
            preferred_element_type=jnp.float32,
        )
        return carry

    lax.fori_loop(0, (live + CHUNK - 1) // CHUNK, step, 0)
    low = acc[:, :WIDTH]
    high = acc[:, WIDTH:]
    lanes = lax.broadcasted_iota(jnp.int32, (rows, WIDTH), 1)
    wide[...] = jnp.where(
        lanes < LB, low + pltpu.roll(low, LB, 1), high + pltpu.roll(high, LB, 1)
    )
    for i in range(IB):
        out[:, i * WIDTH : (i + 1) * WIDTH] = wide[pl.ds(i, nq, stride=IB), :].astype(jnp.bfloat16)


def second(pairs, tiles, count, half, kept, came):
    smem, vmem = pltpu.SMEM, pltpu.VMEM
    rows = half.shape[1]
    return placed(
        second_kernel,
        [smem] * 3 + [vmem] * 3,
        jax.ShapeDtypeStruct((rows // IB, IB * WIDTH), jnp.bfloat16),
        vmem,
        scratch_shapes=[
            pltpu.VMEM((kept.shape[0], WIDTH, WIDTH), jnp.bfloat16),
            pltpu.VMEM((rows, 2 * WIDTH), jnp.float32),
            pltpu.VMEM((rows, WIDTH), jnp.float32),
        ],
        compiler_params=pltpu.CompilerParams(vmem_limit_bytes=16 << 20),
        cost_estimate=pl.CostEstimate(flops=4 << 30, bytes_accessed=4 << 20, transcendentals=0),
    )(pairs, tiles, count, half, kept, came)


def contract_kernel(flat, *refs):
    parts, out = refs[:-1], refs[-1]
    y = member()[1]
    group = y // NL
    nq = flat.shape[0]
    nall = nq * NG
    partial = lax.dot_general(
        jnp.concatenate([p[...] for p in parts], axis=0),
        flat[...],
        (((1,), (1,)), ((), ())),
        preferred_element_type=jnp.float32,
    )
    n = lax.broadcasted_iota(jnp.int32, (nq, WIDTH), 0)
    c = lax.broadcasted_iota(jnp.int32, (nq, WIDTH), 1)
    at = ((n // 2) % NX) * nq + group * (nq // NX) + (n // (2 * NX)) * 2 + n % 2
    lines = [
        jnp.dot(
            partial,
            jnp.where(c == at + f * nall, 1.0, 0.0),
            preferred_element_type=jnp.float32,
            precision=lax.Precision.HIGHEST,
        )
        for f in range(2)
    ]
    for k, hop in enumerate((0,) + HOPS):
        pair = (group + NG - hop) % NG
        for o in range(NL):
            for v in range(NX):
                row = (k * NL + o) * 2 * NX + 2 * v
                out[v * NY + NL * pair + ((y % NL) ^ o)] = (
                    lines[0][row : row + 1, :] + lines[1][row + 1 : row + 2, :]
                )


def contract(flat, parts):
    nall = flat.shape[0] * NG
    return placed(
        contract_kernel,
        [pltpu.VMEM] * (1 + len(parts)),
        jax.ShapeDtypeStruct((nall // 2, 1, 2 * nall), jnp.float32),
        pltpu.VMEM,
        compiler_params=pltpu.CompilerParams(vmem_limit_bytes=4 << 20),
    )(flat, *parts)


def total_kernel(parts, out):
    out[...] = jnp.broadcast_to(jnp.sum(parts[...], axis=0, keepdims=True), out.shape)


def total(parts, copies):
    return placed(
        total_kernel,
        [pltpu.VMEM],
        jax.ShapeDtypeStruct((copies,) + parts.shape[1:], parts.dtype),
        pltpu.VMEM,
        compiler_params=pltpu.CompilerParams(vmem_limit_bytes=1 << 20),
    )(parts)


def finish_kernel(parts, factor, out):
    line = jnp.sum(parts[...], axis=0) * factor[...]
    n = out.shape[1]
    out[0:1, :] = line[:, :n]
    out[1:2, :] = line[:, n:]


def finish(parts, factor):
    return placed(
        finish_kernel,
        [pltpu.VMEM, pltpu.VMEM],
        jax.ShapeDtypeStruct((2, parts.shape[2] // 2), parts.dtype),
        pltpu.VMEM,
        compiler_params=pltpu.CompilerParams(vmem_limit_bytes=1 << 20),
    )(parts, factor)


def per_device(
    occ_tiles,
    vir_tiles,
    three_index,
    send_lists,
    term_pairs,
    term_tiles,
    term_count,
    z_pattern,
    laplace_point,
):
    regions = lax.axis_size("region")
    width = occ_tiles.shape[1]
    per_aux = three_index.shape[1]
    nterms = term_pairs.shape[1]
    x, y = member()

    outgoing = pick(send_lists[0], occ_tiles, vir_tiles, regions)
    recv = lax.all_to_all(outgoing, "region", 0, 0, tiled=True)

    own = lax.all_gather(three_index, "aux", axis=0, tiled=False, axis_index_groups=X_GROUPS)
    def sliced(b, side):
        b = lax.dynamic_slice_in_dim(b, x * IB, IB, 3)
        b = lax.dynamic_slice_in_dim(b, side * LB, LB, 4)
        b = jnp.concatenate([b[:, 0], b[:, 1]], axis=3)
        return b.reshape(NX * per_aux, IB * WIDTH)

    theirs = lax.ppermute(sliced(own, 1 - y % NL), "aux", OTHER)
    late, theirs = lax.optimization_barrier((own, theirs))
    other = lax.ppermute(late, "aux", OTHER)
    part = jnp.concatenate([sliced(own, y % NL), theirs])
    parts = [part] + [lax.ppermute(part, "aux", onward(hop)) for hop in HOPS]

    mask_row = jnp.repeat(z_pattern[0], per_aux).astype(jnp.float32)
    weight = 0.5 + 0.125 * laplace_point[0].astype(jnp.float32)
    scale = weight / (width * jnp.sqrt(jnp.float32(regions * nterms)))
    factor = jnp.concatenate([mask_row, mask_row])[None] * scale

    came = lax.ppermute(recv[:, 2 * IB :, :], "aux", X_OTHER)
    half = first(recv, own, other)
    half, factor = lax.optimization_barrier((half, factor))
    flat = second(term_pairs[0].T, term_tiles[0].T, term_count, half, recv, came)
    partial = contract(flat, parts)

    spread = lax.all_to_all(partial, "aux", 0, 0, tiled=True)
    every = lax.all_to_all(total(spread, regions), "region", 0, 0, tiled=True)
    return finish(every, factor)


def solution(mesh):
    in_specs = (
        P("region", None, None),
        P("region", None, None),
        P("region", "aux", None, None),
        P("region", None, None),
        P("region", None, None),
        P("region", None, None),
        P("region"),
        P("aux", None),
        P(),
    )
    out_specs = P("aux", None)
    return jax.shard_map(
        per_device, mesh=mesh, in_specs=in_specs, out_specs=out_specs, check_vma=False
    )
```

```python
import jax
import jax.numpy as jnp
from jax import lax
from jax.experimental import pallas as pl
from jax.experimental.pallas import tpu as pltpu
from jax.sharding import PartitionSpec as P

NX = 4
NY = 8
NI = 4
NL = 2
NG = NY // NL
WIDTH = 128
IB = WIDTH // NI
LB = WIDTH // NL
KB = WIDTH // 2
X_GROUPS = [[x * NY + y for x in range(NX)] for y in range(NY)]
OTHER = [(x * NY + y, x * NY + (y ^ 1)) for x in range(NX) for y in range(NY)]
X_OTHER = [(x * NY + y, (x ^ 1) * NY + y) for x in range(NX) for y in range(NY)]
HOPS = (2, 1, NG - 1)


def onward(hop):
    return [(x * NY + y, x * NY + (y + NL * hop) % NY) for x in range(NX) for y in range(NY)]


def placed(body, ins, outs, space, **extra):
    return pl.pallas_call(
        body,
        out_shape=outs,
        in_specs=[pl.BlockSpec(memory_space=m) for m in ins],
        out_specs=pl.BlockSpec(memory_space=space),
        **extra,
    )


def member():
    aux = lax.axis_index("aux")
    return aux // NY, aux % NY


PARTS = 4


def pick_kernel(lists, occ, vir, out, rows, tiles, staged, sems):
    x, y = member()
    row = pl.multiple_of(x * IB, IB)
    col = (y % NL) * LB
    depth = pl.multiple_of((x % 2) * KB, KB)
    ntile = occ.shape[0]
    copies = [pltpu.make_async_copy(occ.at[:, pl.ds(row, IB), :], rows, sems.at[0])]
    step = ntile // PARTS
    for u in range(PARTS):
        at = pl.ds(u * step, step)
        copies.append(pltpu.make_async_copy(vir.at[at, pl.ds(depth, KB), :], tiles.at[at], sems.at[1 + u]))
    for c in copies:
        c.start()
    r = lax.broadcasted_iota(jnp.int32, (2 * WIDTH, WIDTH), 0)
    c = lax.broadcasted_iota(jnp.int32, (2 * WIDTH, WIDTH), 1)
    wanted = jnp.where(c < LB, c + col, c - LB + WIDTH + col)
    select = jnp.where(r == wanted, 1.0, 0.0).astype(jnp.bfloat16)
    for c in copies:
        c.wait()
    regions = staged.shape[0]
    step = regions // PARTS
    sent = []
    for u in range(PARTS):
        for d in range(u * step, (u + 1) * step):
            for j in range(2):
                staged[d, j * IB : (j + 1) * IB, :] = rows[lists[0, 2 * d + j]]
            pair = jnp.concatenate([tiles[lists[1, 2 * d]], tiles[lists[1, 2 * d + 1]]], axis=1)
            staged[d, 2 * IB :, :] = jnp.dot(
                pair, select, preferred_element_type=jnp.float32
            ).astype(jnp.bfloat16)
        at = pl.ds(u * step, step)
        sent.append(pltpu.make_async_copy(staged.at[at], out.at[at], sems.at[1 + PARTS + u]))
        sent[-1].start()
    for c in sent:
        c.wait()


def pick(lists, occ, vir, regions):
    smem, hbm = pltpu.SMEM, pltpu.HBM
    shape = (regions, 2 * IB + KB, WIDTH)
    return placed(
        pick_kernel,
        [smem, hbm, hbm],
        jax.ShapeDtypeStruct(shape, jnp.bfloat16),
        hbm,
        scratch_shapes=[
            pltpu.VMEM((occ.shape[0], IB, WIDTH), jnp.bfloat16),
            pltpu.VMEM((vir.shape[0], KB, WIDTH), jnp.bfloat16),
            pltpu.VMEM(shape, jnp.bfloat16),
            pltpu.SemaphoreType.DMA((1 + 2 * PARTS,)),
        ],
        compiler_params=pltpu.CompilerParams(vmem_limit_bytes=60 << 20),
        cost_estimate=pl.CostEstimate(flops=40 << 20, bytes_accessed=2 << 20, transcendentals=0),
    )(lists, occ, vir)


GROUP = 2
WIDE = 2
CHUNK = 32


def first_kernel(recv, own, other, half):
    regions = recv.shape[0]
    parity = member()[1] % NL

    def step(n, carry):
        q = n // (NX // WIDE)
        at = (n % (NX // WIDE)) * WIDE
        source = jnp.concatenate(
            [bq[at + v, q, f] for v in range(WIDE) for bq in (own, other) for f in range(2)], axis=1
        )
        for s in range(0, regions, GROUP):
            occ = recv[s : s + GROUP, 0 : 2 * IB, :].reshape(GROUP * 2 * IB, WIDTH)
            res = jnp.dot(occ, source, preferred_element_type=jnp.float32).astype(jnp.bfloat16)
            for v in range(WIDE):
                for o in range(2):
                    for f in range(2):
                        spot = ((parity ^ o) * NX + at + v) * 2 + f
                        start = pl.multiple_of(spot * IB, IB)
                        left = (v * 4 + o * 2 + f) * WIDTH
                        for u in range(2 * GROUP):
                            half[q * (2 * regions) + 2 * s + u, pl.ds(start, IB), :] = res[
                                u * IB : (u + 1) * IB, left : left + WIDTH
                            ]
        return carry

    lax.fori_loop(0, 2 * NX // WIDE, step, 0)


def first(recv, own, other):
    nq = 2 * own.shape[0] * own.shape[2]
    return placed(
        first_kernel,
        [pltpu.VMEM] * 3,
        jax.ShapeDtypeStruct((4 * recv.shape[0], nq * IB, WIDTH), jnp.bfloat16),
        pltpu.VMEM,
        compiler_params=pltpu.CompilerParams(vmem_limit_bytes=4 << 20),
        cost_estimate=pl.CostEstimate(flops=4 << 30, bytes_accessed=4 << 20, transcendentals=0),
    )(recv, own, other)


def second_kernel(pairs, tiles, count, half, kept, came, out, vir, acc, wide):
    regions = kept.shape[0]
    rows = half.shape[1]
    nq = rows // IB
    depth = pl.multiple_of((member()[0] % 2) * KB, KB)
    vir[:, pl.ds(depth, KB), :] = kept[:, 2 * IB :, :]
    vir[:, pl.ds(KB - depth, KB), :] = came[...]

    acc[...] = jnp.zeros_like(acc)
    live = count[0]
    lane = lax.broadcasted_iota(jnp.int32, (WIDTH, 2 * WIDTH), 1) // LB

    def step(n, carry):
        lhs = []
        rhs = []
        for u in range(CHUNK):
            t = n * CHUNK + u
            at = jnp.minimum(t, live - 1)
            b = tiles[1, at]
            side = jnp.where(t < live, pairs[0, at] * NL + b % 2, -1)
            lhs.append(half[pairs[1, at] * (2 * regions) + tiles[0, at]])
            tile = vir[b // 2]
            tile = jnp.concatenate([tile, tile], axis=1)
            rhs.append(jnp.where(lane == side, tile, jnp.zeros_like(tile)))
        acc[...] += jnp.dot(
            jnp.concatenate(lhs, axis=1),
            jnp.concatenate(rhs, axis=0),
            preferred_element_type=jnp.float32,
        )
        return carry

    lax.fori_loop(0, (live + CHUNK - 1) // CHUNK, step, 0)
    low = acc[:, :WIDTH]
    high = acc[:, WIDTH:]
    lanes = lax.broadcasted_iota(jnp.int32, (rows, WIDTH), 1)
    wide[...] = jnp.where(
        lanes < LB, low + pltpu.roll(low, LB, 1), high + pltpu.roll(high, LB, 1)
    )
    for i in range(IB):
        out[:, i * WIDTH : (i + 1) * WIDTH] = wide[pl.ds(i, nq, stride=IB), :].astype(jnp.bfloat16)


def second(pairs, tiles, count, half, kept, came):
    smem, vmem = pltpu.SMEM, pltpu.VMEM
    rows = half.shape[1]
    return placed(
        second_kernel,
        [smem] * 3 + [vmem] * 3,
        jax.ShapeDtypeStruct((rows // IB, IB * WIDTH), jnp.bfloat16),
        vmem,
        scratch_shapes=[
            pltpu.VMEM((kept.shape[0], WIDTH, WIDTH), jnp.bfloat16),
            pltpu.VMEM((rows, 2 * WIDTH), jnp.float32),
            pltpu.VMEM((rows, WIDTH), jnp.float32),
        ],
        compiler_params=pltpu.CompilerParams(vmem_limit_bytes=16 << 20),
        cost_estimate=pl.CostEstimate(flops=1 << 28, bytes_accessed=1 << 20, transcendentals=0),
    )(pairs, tiles, count, half, kept, came)


def contract_kernel(flat, *refs):
    parts, out = refs[:-1], refs[-1]
    y = member()[1]
    group = y // NL
    nq = flat.shape[0]
    nall = nq * NG
    partial = lax.dot_general(
        jnp.concatenate([p[...] for p in parts], axis=0),
        flat[...],
        (((1,), (1,)), ((), ())),
        preferred_element_type=jnp.float32,
    )
    n = lax.broadcasted_iota(jnp.int32, (nq, WIDTH), 0)
    c = lax.broadcasted_iota(jnp.int32, (nq, WIDTH), 1)
    at = ((n // 2) % NX) * nq + group * (nq // NX) + (n // (2 * NX)) * 2 + n % 2
    lines = [
        jnp.dot(
            partial,
            jnp.where(c == at + f * nall, 1.0, 0.0),
            preferred_element_type=jnp.float32,
            precision=lax.Precision.HIGHEST,
        )
        for f in range(2)
    ]
    for k, hop in enumerate((0,) + HOPS):
        pair = (group + NG - hop) % NG
        for o in range(NL):
            for v in range(NX):
                row = (k * NL + o) * 2 * NX + 2 * v
                out[v * NY + NL * pair + ((y % NL) ^ o)] = (
                    lines[0][row : row + 1, :] + lines[1][row + 1 : row + 2, :]
                )


def contract(flat, parts):
    nall = flat.shape[0] * NG
    return placed(
        contract_kernel,
        [pltpu.VMEM] * (1 + len(parts)),
        jax.ShapeDtypeStruct((nall // 2, 1, 2 * nall), jnp.float32),
        pltpu.VMEM,
        compiler_params=pltpu.CompilerParams(vmem_limit_bytes=4 << 20),
    )(flat, *parts)


def total_kernel(parts, out):
    out[...] = jnp.broadcast_to(jnp.sum(parts[...], axis=0, keepdims=True), out.shape)


def total(parts, copies):
    return placed(
        total_kernel,
        [pltpu.VMEM],
        jax.ShapeDtypeStruct((copies,) + parts.shape[1:], parts.dtype),
        pltpu.VMEM,
        compiler_params=pltpu.CompilerParams(vmem_limit_bytes=1 << 20),
    )(parts)


def finish_kernel(parts, factor, out):
    line = jnp.sum(parts[...], axis=0) * factor[...]
    n = out.shape[1]
    out[0:1, :] = line[:, :n]
    out[1:2, :] = line[:, n:]


def finish(parts, factor):
    return placed(
        finish_kernel,
        [pltpu.VMEM, pltpu.VMEM],
        jax.ShapeDtypeStruct((2, parts.shape[2] // 2), parts.dtype),
        pltpu.VMEM,
        compiler_params=pltpu.CompilerParams(vmem_limit_bytes=1 << 20),
    )(parts, factor)


def per_device(
    occ_tiles,
    vir_tiles,
    three_index,
    send_lists,
    term_pairs,
    term_tiles,
    term_count,
    z_pattern,
    laplace_point,
):
    regions = lax.axis_size("region")
    width = occ_tiles.shape[1]
    per_aux = three_index.shape[1]
    nterms = term_pairs.shape[1]
    x, y = member()

    outgoing = pick(send_lists[0], occ_tiles, vir_tiles, regions)
    recv = lax.all_to_all(outgoing, "region", 0, 0, tiled=True)

    own = lax.all_gather(three_index, "aux", axis=0, tiled=False, axis_index_groups=X_GROUPS)
    def sliced(b, side):
        b = lax.dynamic_slice_in_dim(b, x * IB, IB, 3)
        b = lax.dynamic_slice_in_dim(b, side * LB, LB, 4)
        b = jnp.concatenate([b[:, 0], b[:, 1]], axis=3)
        return b.reshape(NX * per_aux, IB * WIDTH)

    theirs = lax.ppermute(sliced(own, 1 - y % NL), "aux", OTHER)
    late, theirs = lax.optimization_barrier((own, theirs))
    other = lax.ppermute(late, "aux", OTHER)
    part = jnp.concatenate([sliced(own, y % NL), theirs])
    came, late = lax.optimization_barrier((recv[:, 2 * IB :, :], part))
    came = lax.ppermute(came, "aux", X_OTHER)
    parts = [part] + [lax.ppermute(part, "aux", onward(hop)) for hop in HOPS[:2]]
    parts.append(lax.ppermute(late, "aux", onward(HOPS[2])))

    mask_row = jnp.repeat(z_pattern[0], per_aux).astype(jnp.float32)
    weight = 0.5 + 0.125 * laplace_point[0].astype(jnp.float32)
    scale = weight / (width * jnp.sqrt(jnp.float32(regions * nterms)))
    factor = jnp.concatenate([mask_row, mask_row])[None] * scale

    half = first(recv, own, other)
    half, factor = lax.optimization_barrier((half, factor))
    flat = second(term_pairs[0].T, term_tiles[0].T, term_count, half, recv, came)
    partial = contract(flat, parts)

    spread = lax.all_to_all(partial, "aux", 0, 0, tiled=True)
    every = lax.all_to_all(total(spread, regions), "region", 0, 0, tiled=True)
    return finish(every, factor)


def solution(mesh):
    in_specs = (
        P("region", None, None),
        P("region", None, None),
        P("region", "aux", None, None),
        P("region", None, None),
        P("region", None, None),
        P("region", None, None),
        P("region"),
        P("aux", None),
        P(),
    )
    out_specs = P("aux", None)
    return jax.shard_map(
        per_device, mesh=mesh, in_specs=in_specs, out_specs=out_specs, check_vma=False
    )
```

```python
import jax
import jax.numpy as jnp
from jax import lax
from jax.experimental import pallas as pl
from jax.experimental.pallas import tpu as pltpu
from jax.sharding import PartitionSpec as P

NX = 4
NY = 8
NI = 4
NL = 2
NG = NY // NL
WIDTH = 128
IB = WIDTH // NI
LB = WIDTH // NL
KB = WIDTH // 2
X_GROUPS = [[x * NY + y for x in range(NX)] for y in range(NY)]
OTHER = [(x * NY + y, x * NY + (y ^ 1)) for x in range(NX) for y in range(NY)]
X_OTHER = [(x * NY + y, (x ^ 1) * NY + y) for x in range(NX) for y in range(NY)]
HOPS = (2, 1, NG - 1)


def onward(hop):
    return [(x * NY + y, x * NY + (y + NL * hop) % NY) for x in range(NX) for y in range(NY)]


def placed(body, ins, outs, space, **extra):
    return pl.pallas_call(
        body,
        out_shape=outs,
        in_specs=[pl.BlockSpec(memory_space=m) for m in ins],
        out_specs=pl.BlockSpec(memory_space=space),
        **extra,
    )


def member():
    aux = lax.axis_index("aux")
    return aux // NY, aux % NY


PARTS = 4


def pick_kernel(lists, occ, vir, out, rows, tiles, cut, staged, sems):
    x, y = member()
    row = pl.multiple_of(x * IB, IB)
    col = (y % NL) * LB
    depth = pl.multiple_of((x % 2) * KB, KB)
    ntile = occ.shape[0]
    copies = [pltpu.make_async_copy(occ.at[:, pl.ds(row, IB), :], rows, sems.at[0])]
    step = ntile // PARTS
    for u in range(PARTS):
        at = pl.ds(u * step, step)
        copies.append(pltpu.make_async_copy(vir.at[at, pl.ds(depth, KB), :], tiles.at[at], sems.at[1 + u]))
    for c in copies:
        c.start()
    r = lax.broadcasted_iota(jnp.int32, (WIDTH, WIDTH), 0)
    c = lax.broadcasted_iota(jnp.int32, (WIDTH, WIDTH), 1)
    twice = jnp.where(r == c % LB + col, 1.0, 0.0).astype(jnp.bfloat16)
    lane = lax.broadcasted_iota(jnp.int32, (KB, WIDTH), 1)
    for c in copies:
        c.wait()
    cut[...] = (
        jnp.dot(tiles[...].reshape(ntile * KB, WIDTH), twice, preferred_element_type=jnp.float32)
        .astype(jnp.bfloat16)
        .reshape(ntile, KB, WIDTH)
    )
    regions = staged.shape[0]
    step = regions // PARTS
    sent = []
    for u in range(PARTS):
        for d in range(u * step, (u + 1) * step):
            for j in range(2):
                staged[d, j * IB : (j + 1) * IB, :] = rows[lists[0, 2 * d + j]]
            staged[d, 2 * IB :, :] = jnp.where(
                lane < LB, cut[lists[1, 2 * d]], cut[lists[1, 2 * d + 1]]
            )
        at = pl.ds(u * step, step)
        sent.append(pltpu.make_async_copy(staged.at[at], out.at[at], sems.at[1 + PARTS + u]))
        sent[-1].start()
    for c in sent:
        c.wait()


def pick(lists, occ, vir, regions):
    smem, hbm = pltpu.SMEM, pltpu.HBM
    shape = (regions, 2 * IB + KB, WIDTH)
    return placed(
        pick_kernel,
        [smem, hbm, hbm],
        jax.ShapeDtypeStruct(shape, jnp.bfloat16),
        hbm,
        scratch_shapes=[
            pltpu.VMEM((occ.shape[0], IB, WIDTH), jnp.bfloat16),
            pltpu.VMEM((vir.shape[0], KB, WIDTH), jnp.bfloat16),
            pltpu.VMEM((vir.shape[0], KB, WIDTH), jnp.bfloat16),
            pltpu.VMEM(shape, jnp.bfloat16),
            pltpu.SemaphoreType.DMA((1 + 2 * PARTS,)),
        ],
        compiler_params=pltpu.CompilerParams(vmem_limit_bytes=60 << 20),
        cost_estimate=pl.CostEstimate(flops=40 << 20, bytes_accessed=2 << 20, transcendentals=0),
    )(lists, occ, vir)


GROUP = 2
WIDE = 4
CHUNK = 32


def first_kernel(recv, own, other, half):
    regions = recv.shape[0]
    parity = member()[1] % NL

    def step(n, carry):
        q = n // (NX // WIDE)
        at = (n % (NX // WIDE)) * WIDE
        source = jnp.concatenate(
            [bq[at + v, q, f] for v in range(WIDE) for bq in (own, other) for f in range(2)], axis=1
        )
        for s in range(0, regions, GROUP):
            occ = recv[s : s + GROUP, 0 : 2 * IB, :].reshape(GROUP * 2 * IB, WIDTH)
            res = jnp.dot(occ, source, preferred_element_type=jnp.float32).astype(jnp.bfloat16)
            for v in range(WIDE):
                for o in range(2):
                    for f in range(2):
                        spot = ((parity ^ o) * NX + at + v) * 2 + f
                        start = pl.multiple_of(spot * IB, IB)
                        left = (v * 4 + o * 2 + f) * WIDTH
                        for u in range(2 * GROUP):
                            half[q * (2 * regions) + 2 * s + u, pl.ds(start, IB), :] = res[
                                u * IB : (u + 1) * IB, left : left + WIDTH
                            ]
        return carry

    lax.fori_loop(0, 2 * NX // WIDE, step, 0)


def first(recv, own, other):
    nq = 2 * own.shape[0] * own.shape[2]
    return placed(
        first_kernel,
        [pltpu.VMEM] * 3,
        jax.ShapeDtypeStruct((4 * recv.shape[0], nq * IB, WIDTH), jnp.bfloat16),
        pltpu.VMEM,
        compiler_params=pltpu.CompilerParams(vmem_limit_bytes=4 << 20),
        cost_estimate=pl.CostEstimate(flops=4 << 30, bytes_accessed=4 << 20, transcendentals=0),
    )(recv, own, other)


def second_kernel(pairs, tiles, count, half, kept, came, out, vir, acc, wide):
    regions = kept.shape[0]
    rows = half.shape[1]
    nq = rows // IB
    depth = pl.multiple_of((member()[0] % 2) * KB, KB)
    vir[:, pl.ds(depth, KB), :] = kept[:, 2 * IB :, :]
    vir[:, pl.ds(KB - depth, KB), :] = came[...]

    acc[...] = jnp.zeros_like(acc)
    live = count[0]
    lane = lax.broadcasted_iota(jnp.int32, (WIDTH, 2 * WIDTH), 1) // LB

    def step(n, carry):
        lhs = []
        rhs = []
        for u in range(CHUNK):
            t = n * CHUNK + u
            at = jnp.minimum(t, live - 1)
            b = tiles[1, at]
            side = jnp.where(t < live, pairs[0, at] * NL + b % 2, -1)
            lhs.append(half[pairs[1, at] * (2 * regions) + tiles[0, at]])
            tile = vir[b // 2]
            tile = jnp.concatenate([tile, tile], axis=1)
            rhs.append(jnp.where(lane == side, tile, jnp.zeros_like(tile)))
        acc[...] += jnp.dot(
            jnp.concatenate(lhs, axis=1),
            jnp.concatenate(rhs, axis=0),
            preferred_element_type=jnp.float32,
        )
        return carry

    lax.fori_loop(0, (live + CHUNK - 1) // CHUNK, step, 0)
    low = acc[:, :WIDTH]
    high = acc[:, WIDTH:]
    lanes = lax.broadcasted_iota(jnp.int32, (rows, WIDTH), 1)
    wide[...] = jnp.where(
        lanes < LB, low + pltpu.roll(low, LB, 1), high + pltpu.roll(high, LB, 1)
    )
    for i in range(IB):
        out[:, i * WIDTH : (i + 1) * WIDTH] = wide[pl.ds(i, nq, stride=IB), :].astype(jnp.bfloat16)


def second(pairs, tiles, count, half, kept, came):
    smem, vmem = pltpu.SMEM, pltpu.VMEM
    rows = half.shape[1]
    return placed(
        second_kernel,
        [smem] * 3 + [vmem] * 3,
        jax.ShapeDtypeStruct((rows // IB, IB * WIDTH), jnp.bfloat16),
        vmem,
        scratch_shapes=[
            pltpu.VMEM((kept.shape[0], WIDTH, WIDTH), jnp.bfloat16),
            pltpu.VMEM((rows, 2 * WIDTH), jnp.float32),
            pltpu.VMEM((rows, WIDTH), jnp.float32),
        ],
        compiler_params=pltpu.CompilerParams(vmem_limit_bytes=16 << 20),
        cost_estimate=pl.CostEstimate(flops=1 << 28, bytes_accessed=1 << 20, transcendentals=0),
    )(pairs, tiles, count, half, kept, came)


def contract_kernel(flat, *refs):
    parts, out = refs[:-1], refs[-1]
    y = member()[1]
    group = y // NL
    nq = flat.shape[0]
    nall = nq * NG
    partial = lax.dot_general(
        jnp.concatenate([p[...] for p in parts], axis=0),
        flat[...],
        (((1,), (1,)), ((), ())),
        preferred_element_type=jnp.float32,
    )
    n = lax.broadcasted_iota(jnp.int32, (nq, WIDTH), 0)
    c = lax.broadcasted_iota(jnp.int32, (nq, WIDTH), 1)
    at = ((n // 2) % NX) * nq + group * (nq // NX) + (n // (2 * NX)) * 2 + n % 2
    lines = [
        jnp.dot(
            partial,
            jnp.where(c == at + f * nall, 1.0, 0.0),
            preferred_element_type=jnp.float32,
            precision=lax.Precision.HIGHEST,
        )
        for f in range(2)
    ]
    for k, hop in enumerate((0,) + HOPS):
        pair = (group + NG - hop) % NG
        for o in range(NL):
            for v in range(NX):
                row = (k * NL + o) * 2 * NX + 2 * v
                out[v * NY + NL * pair + ((y % NL) ^ o)] = (
                    lines[0][row : row + 1, :] + lines[1][row + 1 : row + 2, :]
                )


def contract(flat, parts):
    nall = flat.shape[0] * NG
    return placed(
        contract_kernel,
        [pltpu.VMEM] * (1 + len(parts)),
        jax.ShapeDtypeStruct((nall // 2, 1, 2 * nall), jnp.float32),
        pltpu.VMEM,
        compiler_params=pltpu.CompilerParams(vmem_limit_bytes=4 << 20),
    )(flat, *parts)


def total_kernel(parts, out):
    out[...] = jnp.broadcast_to(jnp.sum(parts[...], axis=0, keepdims=True), out.shape)


def total(parts, copies):
    return placed(
        total_kernel,
        [pltpu.VMEM],
        jax.ShapeDtypeStruct((copies,) + parts.shape[1:], parts.dtype),
        pltpu.VMEM,
        compiler_params=pltpu.CompilerParams(vmem_limit_bytes=1 << 20),
    )(parts)


def finish_kernel(parts, factor, out):
    line = jnp.sum(parts[...], axis=0) * factor[...]
    n = out.shape[1]
    out[0:1, :] = line[:, :n]
    out[1:2, :] = line[:, n:]


def finish(parts, factor):
    return placed(
        finish_kernel,
        [pltpu.VMEM, pltpu.VMEM],
        jax.ShapeDtypeStruct((2, parts.shape[2] // 2), parts.dtype),
        pltpu.VMEM,
        compiler_params=pltpu.CompilerParams(vmem_limit_bytes=1 << 20),
    )(parts, factor)


def per_device(
    occ_tiles,
    vir_tiles,
    three_index,
    send_lists,
    term_pairs,
    term_tiles,
    term_count,
    z_pattern,
    laplace_point,
):
    regions = lax.axis_size("region")
    width = occ_tiles.shape[1]
    per_aux = three_index.shape[1]
    nterms = term_pairs.shape[1]
    x, y = member()

    outgoing = pick(send_lists[0], occ_tiles, vir_tiles, regions)
    recv = lax.all_to_all(outgoing, "region", 0, 0, tiled=True)

    own = lax.all_gather(three_index, "aux", axis=0, tiled=False, axis_index_groups=X_GROUPS)
    def sliced(b, side):
        b = lax.dynamic_slice_in_dim(b, x * IB, IB, 3)
        b = lax.dynamic_slice_in_dim(b, side * LB, LB, 4)
        b = jnp.concatenate([b[:, 0], b[:, 1]], axis=3)
        return b.reshape(NX * per_aux, IB * WIDTH)

    theirs = lax.ppermute(sliced(own, 1 - y % NL), "aux", OTHER)
    late, theirs = lax.optimization_barrier((own, theirs))
    other = lax.ppermute(late, "aux", OTHER)
    part = jnp.concatenate([sliced(own, y % NL), theirs])
    came, late = lax.optimization_barrier((recv[:, 2 * IB :, :], part))
    came = lax.ppermute(came, "aux", X_OTHER)
    parts = [part] + [lax.ppermute(part, "aux", onward(hop)) for hop in HOPS[:2]]
    parts.append(lax.ppermute(late, "aux", onward(HOPS[2])))

    mask_row = jnp.repeat(z_pattern[0], per_aux).astype(jnp.float32)
    weight = 0.5 + 0.125 * laplace_point[0].astype(jnp.float32)
    scale = weight / (width * jnp.sqrt(jnp.float32(regions * nterms)))
    factor = jnp.concatenate([mask_row, mask_row])[None] * scale

    half = first(recv, own, other)
    half, factor = lax.optimization_barrier((half, factor))
    flat = second(term_pairs[0].T, term_tiles[0].T, term_count, half, recv, came)
    partial = contract(flat, parts)

    spread = lax.all_to_all(partial, "aux", 0, 0, tiled=True)
    every = lax.all_to_all(total(spread, regions), "region", 0, 0, tiled=True)
    return finish(every, factor)


def solution(mesh):
    in_specs = (
        P("region", None, None),
        P("region", None, None),
        P("region", "aux", None, None),
        P("region", None, None),
        P("region", None, None),
        P("region", None, None),
        P("region"),
        P("aux", None),
        P(),
    )
    out_specs = P("aux", None)
    return jax.shard_map(
        per_device, mesh=mesh, in_specs=in_specs, out_specs=out_specs, check_vma=False
    )
```
